128 devices in a mesh: dp: 2 (over x_lo), seq: 16 (over z, y), mp: 4 (over x_hi, core).
Axes of the slice: x: 4 (x_hi: 2, x_lo: 2; x = x_hi * 2 + x_lo), y: 4, z: 4, core: 2. Of those that a mesh axis runs over, the one named last changes fastest.
Arguments:
- shortening_input: bfloat16 [2, 32768, 2048], P('dp', ('seq', 'mp')), may hold values from -16 to 16
- coarse_grad: bfloat16 [2, 8192, 4096], P('dp', 'seq', 'mp'), may hold values from -6 to 6
- weight_copy: bfloat16 [2, 4096, 4096], P('dp', None, 'mp'), may hold values from -0.0625 to 0.0625
- master: float32 [2, 4096, 4096], P('dp', 'seq', 'mp'), may hold values from -3 to 3
- moment: float32 [2, 4096, 4096], P('dp', 'seq', 'mp'), may hold values from -3 to 3
- second: float32 [2, 4096, 4096], P('dp', 'seq', 'mp'), may hold values from 0.05 to 5
Outputs:
- act_grad: bfloat16 [2, 32768, 2048], P('dp', ('seq', 'mp'))
- new_master: float32 [2, 4096, 4096], P('dp', 'seq', 'mp')
- new_moment: float32 [2, 4096, 4096], P('dp', 'seq', 'mp')
- new_second: float32 [2, 4096, 4096], P('dp', 'seq', 'mp')
- new_weight: bfloat16 [2, 4096, 4096], P(None, 'seq', 'mp')
The draws below stay inside these ranges and needn't reach their ends.
All inputs are finite; a program needn't handle non-finite values.
Results may differ from the reference program's by a relative error of at most 0.009.
Values may be sent and summed in bfloat16 or wider, within the bound.
A program may use at most 128 MiB of HBM per device.

```python
import math
import jax
import jax.numpy as jnp
from jax import lax

DF = 2048
DC = 4096
SHORT = 4
BATCH = 2
SEQ_LEN = 32768
COARSE = 8192
N_DP = 2
N_SEQ = 16
N_MP = 4


def raised(values, key, source, target, parts, factor):
    def block_of(position):
        return (jnp.arange(values.shape[position]) // (values.shape[position] // parts)).reshape((-1,) + (1,) * (values.ndim - 1 - position))

    one_side = jax.random.permutation(key, parts)[block_of(target)]
    far = (block_of(target) + parts // 2) % parts
    return jnp.where((block_of(source) == one_side) | (block_of(source) == far), factor * values, values)


def levels(own_key, extent, shards, smallest, largest):
    def one(dim, shards_of):
        draws = jax.random.uniform(jax.random.fold_in(jax.random.fold_in(own_key, 6), dim), (shards_of,), jnp.float32, smallest / len(shards), largest / len(shards))
        return jnp.repeat(jnp.exp(draws), extent[dim] // shards_of).reshape((-1,) + (1,) * (len(extent) - dim - 1))

    loudness = one(*shards[0])
    for cut in shards[1:]:
        loudness = loudness * one(*cut)
    return loudness


def centred(own_key, dims, deviation, reach, split=(), held_as=jnp.bfloat16):
    result = jax.random.normal(own_key, dims, jnp.float32) * deviation
    if len(split) > 0:
        result = levels(own_key, dims, split, -0.22, 0.18) * result
    return jnp.clip(result, min=-reach, max=reach).astype(held_as)


def heavy_noise(rng, shape, scale, bound, split, heavy, kind=jnp.bfloat16):
    array = scale * jax.random.normal(rng, shape, jnp.float32)
    if split:
        array = array * levels(rng, shape, split, -0.22, 0.18)
    return jnp.clip(raised(array, jax.random.fold_in(rng, 3), *heavy), -bound, bound).astype(kind)


def setup_inputs(seed: int = 0) -> dict:
    arg_keys = jax.random.split(jax.random.key(seed), 7)
    return {
        "shortening_input": heavy_noise(arg_keys[0], (BATCH, SEQ_LEN, DF), 1.0, 16.0, ((0, 2), (1, 64)), (1, 2, 64, 4.0)),
        "coarse_grad": centred(arg_keys[1], (BATCH, COARSE, DC), 1.0, 6.0, ((0, 2), (1, 16), (2, 4))),
        "weight_copy": centred(arg_keys[2], (N_DP, SHORT * DF // N_DP, DC), (SHORT * DF) ** -0.5, 0.0625, ((0, 2), (2, 4))),
        "master": centred(arg_keys[3], (N_DP, SHORT * DF // N_DP, DC), 0.5, 3.0, ((0, 2), (1, 16), (2, 4)), jnp.float32),
        "moment": centred(arg_keys[4], (N_DP, SHORT * DF // N_DP, DC), 0.5, 3.0, ((0, 2), (1, 16), (2, 4)), jnp.float32),
        "second": jnp.clip(jnp.exp(math.log(5.0) - 4.6051702 * jax.random.uniform(arg_keys[5], (N_DP, SHORT * DF // N_DP, DC), jnp.float32) ** levels(arg_keys[5], (N_DP, SHORT * DF // N_DP, DC), ((0, 2), (1, 16), (2, 4)), -0.2, 0.2)), 0.05, 5.0),
    }


first_beta = 0.9
second_beta = 0.95
first_fix = 1.0 - 0.9 ** 10
second_fix = 1.0 - 0.95 ** 10
adam_eps = 1e-08
learn_rate = 0.05
weight_decay = 0.1

def reference(shortening_input, coarse_grad, weight_copy, master, moment, second):
    sequences = shortening_input.shape[0]
    wide_rows = SHORT * DF
    weights = weight_copy.reshape(wide_rows, DC)
    width = DC // N_MP
    grad_matrix = coarse_grad.reshape(sequences * COARSE, DC)
    accum = jnp.zeros((sequences * COARSE, wide_rows), jnp.float32)
    for block in range(N_MP):
        grad_block = grad_matrix[:, block * width:(block + 1) * width]
        weight_block = weights[:, block * width:(block + 1) * width]
        partial_sum = lax.dot_general(grad_block, weight_block, (((1,), (1,)), ((), ())), preferred_element_type=jnp.float32)
        rounded = lax.optimization_barrier(partial_sum.astype(jnp.bfloat16))
        accum = accum + rounded.astype(jnp.float32)
    fine_grad = accum.reshape(sequences, SEQ_LEN, DF)
    tail_zeros = jnp.zeros((sequences, SHORT - 1, DF), jnp.float32)
    act_grad = jnp.concatenate([fine_grad[:, SHORT - 1:], tail_zeros], axis=1).astype(jnp.bfloat16)
    inputs = shortening_input.reshape(sequences * COARSE, wide_rows)
    block_rows = COARSE // N_SEQ
    block_count = sequences * N_SEQ

    def add_block(index, total):
        start = (index * block_rows).astype(jnp.int32)
        picked = lax.dynamic_slice_in_dim(inputs, start, block_rows, 0)
        grads = lax.dynamic_slice_in_dim(grad_matrix, start, block_rows, 0)
        term = lax.dot_general(picked, grads, (((0,), (0,)), ((), ())), preferred_element_type=jnp.float32)
        rounded = lax.optimization_barrier(term.astype(jnp.bfloat16))
        return total + rounded.astype(jnp.float32)
    summed = lax.fori_loop(0, block_count, add_block, jnp.zeros((wide_rows, DC), jnp.float32))
    weight_grad = (summed * (1.0 / math.sqrt(sequences * COARSE))).reshape(master.shape)
    new_moment = first_beta * moment + (1.0 - first_beta) * weight_grad
    new_second = second_beta * second + (1.0 - second_beta) * weight_grad * weight_grad
    step_ratio = new_moment / first_fix / (jnp.sqrt(new_second / second_fix) + adam_eps)
    new_master = master - learn_rate * (step_ratio + weight_decay * master)
    new_weight = new_master.astype(jnp.bfloat16)
    return (act_grad, new_master, new_moment, new_second, new_weight)
```

```python
import functools
import math

import jax
import jax.numpy as jnp
from jax import lax
from jax.experimental import pallas as pl
from jax.experimental.pallas import tpu as pltpu
from jax.sharding import PartitionSpec as P

MESH = pl.DeviceIdType.MESH
SHORT = 4
SIDE = 4

first_beta = 0.9
second_beta = 0.95
first_fix = 1.0 - 0.9**10
second_fix = 1.0 - 0.95**10
adam_eps = 1e-08
learn_rate = 0.05
weight_decay = 0.1

COPIES = 80
LOCALS = 16

F32 = jnp.float32
BF16 = jnp.bfloat16


def kernel(
    scale, x_hbm, g_hbm, w_hbm, ma_hbm, mo_hbm, se_hbm,
    act_hbm, nm_hbm, nmo_hbm, ns_hbm, nw_hbm,
    xf, xall, x2t, xrel, g2, g2s, wown, wsib, pbuf, actr, arel, rbuf,
    dwp, r1, r2, st, r3, r4, ma, mo, se, nwb, bsend, brecv,
    send_sem, recv_sem, local_sem,
):
    d = lax.axis_index("dp")
    s = lax.axis_index("seq")
    m = lax.axis_index("mp")
    z, y = s // SIDE, s % SIDE
    h, c = m // 2, m % 2
    od, oh, oc = 1 - d, 1 - h, 1 - c

    def near(dd, hh, cc):
        return {"dp": dd, "mp": 2 * hh + cc}

    def slot(dd, hh, cc):
        return 4 * dd + 2 * hh + cc

    me = slot(d, h, c)
    sibling = near(d, h, oc)
    intra, intra_o = near(od, h, c), near(od, h, oc)
    inter, inter_o = near(od, oh, c), near(od, oh, oc)

    def at_seq(zz, yy):
        return {"seq": zz * SIDE + yy}

    up = lambda v: (v + 1) % SIDE
    down = lambda v: (v + SIDE - 1) % SIDE
    across = lambda v: (v + 2) % SIDE
    zp, zm = at_seq(up(z), y), at_seq(down(z), y)
    yp, ym = at_seq(z, up(y)), at_seq(z, down(y))
    total = 64
    place = s * 4 + m
    before = (place + total - 1) % total
    after = (place + 1) % total
    prev_dev = {"seq": before // 4, "mp": before % 4}
    next_dev = {"seq": after // 4, "mp": after % 4}

    sent, ids, local_ids = [], {}, {}

    def send(name, src, dst, device):
        i = ids.setdefault(name, len(ids))
        copy = pltpu.make_async_remote_copy(
            src_ref=src, dst_ref=dst, send_sem=send_sem.at[i], recv_sem=recv_sem.at[i],
            device_id=device, device_id_type=MESH,
        )
        copy.start()
        sent.append(copy)

    def arrived(name, dst):
        i = ids.setdefault(name, len(ids))
        pltpu.make_async_remote_copy(
            src_ref=dst, dst_ref=dst, send_sem=send_sem.at[i], recv_sem=recv_sem.at[i],
            device_id=sibling, device_id_type=MESH,
        ).wait_recv()

    def local(name, src, dst):
        copy = pltpu.make_async_copy(src, dst, local_sem.at[local_ids.setdefault(name, len(local_ids))])
        copy.start()
        return copy

    in_x = local("x", x_hbm, xf)
    in_g = local("g", g_hbm, g2.at[d])
    in_w = local("w", w_hbm.at[c], wown)
    in_ma = local("ma", ma_hbm, ma)
    in_mo = local("mo", mo_hbm, mo)
    in_se = local("se", se_hbm, se)

    barrier = pltpu.get_barrier_semaphore()
    partners = (sibling, intra, intra_o, inter, inter_o, zp, zm, yp, ym, prev_dev, next_dev)
    for device in partners:
        pl.semaphore_signal(barrier, inc=1, device_id=device, device_id_type=MESH)
    pl.semaphore_wait(barrier, len(partners))

    send("G0", g_hbm, g2.at[d], intra)
    send("G1", g_hbm, g2s.at[d], sibling)
    send("W", w_hbm.at[oc], wsib, sibling)

    in_x.wait()

    def turn(i, carry):
        p, tile = i // 4, i % 4
        rows = lax.broadcasted_iota(jnp.int32, (128, 512), 0)
        cols = lax.broadcasted_iota(jnp.int32, (128, 512), 1)
        pick = jnp.where(cols == 4 * rows + p, 1.0, 0.0).astype(BF16)
        got = jnp.dot(pick, xf[:, pl.ds(pl.multiple_of(tile * 512, 512), 512)], preferred_element_type=F32)
        turned = got.T.astype(BF16)
        for j in range(4):
            owner = (p % 2) * 8 + tile * 2 + j // 2
            where = owner if j % 2 == 0 else 16 + (owner % SIDE) * SIDE + owner // SIDE
            for ch in range(2):
                xall[p // 2, ch, where] = turned[j * 128 + ch * 64:j * 128 + ch * 64 + 64]
        return carry

    lax.fori_loop(0, 16, turn, 0)
    own_x = local("xown", xall.at[d], x2t.at[me])
    first, second = pl.ds(0, 16), pl.ds(16, 16)

    def start_x(ch):
        tag = str(ch)
        send("Xa" + tag, xall.at[d, ch, first], xrel.at[ch, 0], intra)
        send("Xb" + tag, xall.at[d, ch, second], xrel.at[ch, 1], inter)
        send("Xd" + tag, xall.at[od, ch], x2t.at[me, ch], inter)
        send("Xc" + tag, xall.at[od, ch], x2t.at[me, ch], intra)
        send("Xe" + tag, xall.at[d, ch], x2t.at[me, ch], sibling)

    def relay_b(ch):
        arrived("Xb" + str(ch), xrel.at[ch, 1])
        send("Xb2" + str(ch), xrel.at[ch, 1], x2t.at[slot(od, oh, c), ch, second], intra)

    def relay_a(ch):
        arrived("Xa" + str(ch), xrel.at[ch, 0])
        send("Xa2" + str(ch), xrel.at[ch, 0], x2t.at[slot(od, h, c), ch, first], inter)

    def pass_on(name, ch, dst):
        arrived(name + str(ch), dst)
        send("F" + name + str(ch), dst, dst, sibling)

    def passed(name, ch, dst):
        arrived("F" + name + str(ch), dst)

    def act_half(dd):
        def step(t, carry):
            outs = pl.ds(pl.multiple_of(t * 256, 256), 256)
            dims = (((1,), (1,)), ((), ()))
            part = lax.dot_general(g2[dd], wown[outs, :], dims, preferred_element_type=F32)
            part += lax.dot_general(g2s[dd], wsib[outs, :], dims, preferred_element_type=F32)
            pbuf[dd, :, :, outs] = part.astype(BF16).reshape(4, 128, 256)
            return carry

        lax.fori_loop(0, 8, step, 0)

    def grad_tile(ch, group_a, group_b):
        tile_a, tile_b = pl.ds(4 * group_a, 4), pl.ds(16 + 4 * group_b, 4)

        def step(t, carry):
            cols = pl.ds(pl.multiple_of(t * 256, 256), 256)
            left = jnp.concatenate(
                [
                    jnp.concatenate([x2t[k, ch, tile].reshape(256, 128) for k in range(8)], axis=1)
                    for tile in (tile_a, tile_b)
                ],
                axis=0,
            )
            right = jnp.concatenate([g2[0, :, cols], g2[1, :, cols]], axis=0)
            part = jnp.dot(left, right, preferred_element_type=F32).astype(BF16).reshape(2, 4, 64, 256)
            dwp[ch, 0, group_a, :, :, cols] = part[0]
            dwp[ch, 1, group_b, :, :, cols] = part[1]
            return carry

        lax.fori_loop(0, 4, step, 0)

    def wide(v):
        return v.astype(F32)

    halves = (("A", z, y, zp, zm, yp, ym), ("B", y, z, yp, ym, zp, zm))

    def reduce_1(ch):
        for i, (tag, a1, a2, p1, m1, p2, m2) in enumerate(halves):
            tag += str(ch)
            send(tag + "1p", dwp.at[ch, i, across(a1), pl.ds(0, 2)], r1.at[ch, i, 0], p1)
            send(tag + "1m", dwp.at[ch, i, across(a1), pl.ds(2, 2)], r1.at[ch, i, 1], m1)

    def reduce_2(ch):
        for i, (tag, a1, a2, p1, m1, p2, m2) in enumerate(halves):
            tag += str(ch)
            arrived(tag + "1p", r1.at[ch, i, 0])
            for j in range(2):
                dwp[ch, i, up(a1), j] = (wide(dwp[ch, i, up(a1), j]) + wide(r1[ch, i, 0, j])).astype(BF16)
            send(tag + "2p", dwp.at[ch, i, up(a1)], r2.at[ch, i, 0], p1)
            arrived(tag + "1m", r1.at[ch, i, 1])
            for j in range(2):
                dwp[ch, i, down(a1), 2 + j] = (
                    wide(dwp[ch, i, down(a1), 2 + j]) + wide(r1[ch, i, 1, j])
                ).astype(BF16)
            send(tag + "2m", dwp.at[ch, i, down(a1)], r2.at[ch, i, 1], m1)

    def reduce_3(ch):
        for i, (tag, a1, a2, p1, m1, p2, m2) in enumerate(halves):
            tag += str(ch)
            arrived(tag + "2p", r2.at[ch, i, 0])
            arrived(tag + "2m", r2.at[ch, i, 1])
            for j in range(4):
                st[ch, i, j] = (
                    wide(dwp[ch, i, a1, j]) + wide(r2[ch, i, 0, j]) + wide(r2[ch, i, 1, j])
                ).astype(BF16)
            send(tag + "3p", st.at[ch, i, across(a2), pl.ds(0, 32)], r3.at[ch, i, 0], p2)
            send(tag + "3m", st.at[ch, i, across(a2), pl.ds(32, 32)], r3.at[ch, i, 1], m2)

    def reduce_4(ch):
        for i, (tag, a1, a2, p1, m1, p2, m2) in enumerate(halves):
            tag += str(ch)
            arrived(tag + "3p", r3.at[ch, i, 0])
            st[ch, i, up(a2), 0:32] = (wide(st[ch, i, up(a2), 0:32]) + wide(r3[ch, i, 0])).astype(BF16)
            send(tag + "4p", st.at[ch, i, up(a2)], r4.at[ch, i, 0], p2)
            arrived(tag + "3m", r3.at[ch, i, 1])
            st[ch, i, down(a2), 32:64] = (
                wide(st[ch, i, down(a2), 32:64]) + wide(r3[ch, i, 1])
            ).astype(BF16)
            send(tag + "4m", st.at[ch, i, down(a2)], r4.at[ch, i, 1], m2)

    def update(ch):
        for i, (tag, a1, a2, p1, m1, p2, m2) in enumerate(halves):
            tag += str(ch)
            arrived(tag + "4p", r4.at[ch, i, 0])
            arrived(tag + "4m", r4.at[ch, i, 1])
            rows = slice(128 * i + 64 * ch, 128 * i + 64 * ch + 64)
            grad = (wide(st[ch, i, a2]) + wide(r4[ch, i, 0]) + wide(r4[ch, i, 1])) * scale
            new_moment = first_beta * mo[rows, :] + (1.0 - first_beta) * grad
            new_second = second_beta * se[rows, :] + (1.0 - second_beta) * grad * grad
            ratio = new_moment / first_fix / (jnp.sqrt(new_second / second_fix) + adam_eps)
            old = ma[rows, :]
            new_master = old - learn_rate * (ratio + weight_decay * old)
            mo[rows, :] = new_moment
            se[rows, :] = new_second
            ma[rows, :] = new_master
            nwb[i, ch] = new_master.astype(BF16)
        both = pl.ds(0, 2)
        send("nw" + str(ch), nwb.at[both, ch], nw_hbm.at[d, both, ch], intra)

    start_x(0)
    in_g.wait()
    in_w.wait()
    relay_b(0)
    start_x(1)
    arrived("G1", g2s.at[d])
    arrived("W", wsib)
    act_half(d)
    arrived("G0", g2.at[od])
    send("G2", g2.at[od], g2s.at[od], sibling)
    arrived("G2", g2s.at[od])
    act_half(od)
    relay_a(0)
    relay_b(1)

    send("Pd1", pbuf.at[d, 2 * oh + oc], arel.at[1], inter)
    send("Pd0", pbuf.at[d, 2 * oh + c], arel.at[0], intra)
    send("Pb0", pbuf.at[od, 2 * h + c], actr.at[me], intra)
    send("Pb1", pbuf.at[od, 2 * h + oc], actr.at[me], intra_o)
    send("Pa", pbuf.at[d, 2 * h + oc], actr.at[me], sibling)

    def pass_all(ch):
        pass_on("Xd", ch, x2t.at[slot(od, oh, c), ch])
        pass_on("Xc", ch, x2t.at[slot(od, h, c), ch])
        pass_on("Xa2", ch, x2t.at[slot(d, oh, c), ch, first])
        pass_on("Xb2", ch, x2t.at[slot(d, oh, c), ch, second])

    def all_passed(ch):
        arrived("Xe" + str(ch), x2t.at[slot(d, h, oc), ch])
        passed("Xd", ch, x2t.at[slot(od, oh, oc), ch])
        passed("Xc", ch, x2t.at[slot(od, h, oc), ch])
        passed("Xa2", ch, x2t.at[slot(d, oh, oc), ch, first])
        passed("Xb2", ch, x2t.at[slot(d, oh, oc), ch, second])

    pass_all(0)
    own_x.wait()
    all_passed(0)

    grad_tile(0, across(z), across(y))
    reduce_1(0)
    grad_tile(0, up(z), up(y))
    relay_a(1)
    send("Pc0", pbuf.at[od, 2 * oh + c], actr.at[me], inter)
    send("Pc1", pbuf.at[od, 2 * oh + oc], actr.at[me], inter_o)
    grad_tile(0, down(z), down(y))
    grad_tile(0, z, y)
    reduce_2(0)
    arrived("Pd1", arel.at[1])
    send("Pf1", arel.at[1], actr.at[slot(od, oh, c)], intra_o)

    pass_all(1)
    all_passed(1)
    grad_tile(1, across(z), across(y))
    reduce_1(1)
    reduce_3(0)
    grad_tile(1, up(z), up(y))
    grad_tile(1, down(z), down(y))
    reduce_4(0)
    grad_tile(1, z, y)
    reduce_2(1)
    arrived("Pd0", arel.at[0])
    send("Pf0", arel.at[0], actr.at[slot(od, h, c)], inter)
    in_ma.wait()
    in_mo.wait()
    in_se.wait()
    update(0)
    reduce_3(1)
    reduce_4(1)
    update(1)
    outs = [
        local("onw", nwb, nw_hbm.at[d]),
        local("onm", ma, nm_hbm),
        local("onmo", mo, nmo_hbm),
        local("ons", se, ns_hbm),
    ]

    arrived("Pa", actr.at[slot(d, h, oc)])
    arrived("Pb0", actr.at[slot(od, h, c)])
    arrived("Pb1", actr.at[slot(od, h, oc)])
    arrived("Pc0", actr.at[slot(od, oh, c)])
    arrived("Pc1", actr.at[slot(od, oh, oc)])
    arrived("Pf0", actr.at[slot(d, oh, c)])
    arrived("Pf1", actr.at[slot(d, oh, oc)])
    actr[me] = pbuf[d, m]
    for p in range(4):
        k = 4 * (p // 2) + p % 2
        both = wide(actr[k]) + wide(actr[k + 2])
        rbuf[p * 128:(p + 1) * 128, :] = both.astype(BF16)
        bsend[p:p + 1, :] = both[0:1]
    send("bnd", bsend, brecv, prev_dev)
    arrived("bnd", brecv)
    last = place == total - 1
    rows = lax.broadcasted_iota(jnp.int32, (512, 512), 0)
    cols = lax.broadcasted_iota(jnp.int32, (512, 512), 1)
    put = jnp.where(rows == 4 * (cols % 128) + cols // 128 - 3, 1.0, 0.0).astype(BF16)

    def finish(t, carry):
        span = pl.ds(pl.multiple_of(t * 512, 512), 512)
        out = jnp.dot(put, rbuf[:, span], preferred_element_type=F32)
        xf[0:496, span] = out[0:496].astype(BF16)
        tail = out[496:512]
        line = lax.broadcasted_iota(jnp.int32, (16, 512), 0)
        for p in range(3):
            row = jnp.where(last, 0.0, brecv[p:p + 1, span])
            tail = jnp.where(line == 13 + p, row, tail)
        xf[496:512, span] = tail.astype(BF16)
        return carry

    lax.fori_loop(0, 4, finish, 0)
    outs.append(local("oact", xf, act_hbm))
    for ch in range(2):
        arrived("nw" + str(ch), nw_hbm.at[od, pl.ds(0, 2), ch])
    for copy in outs:
        copy.wait()
    for copy in sent:
        copy.wait_send()


def per_device(shortening_input, coarse_grad, weight_copy, master, moment, second):
    x = shortening_input[0]
    g = coarse_grad[0]
    fine, features = x.shape
    width = g.shape[1]
    w = weight_copy.reshape(2, features, width)
    rows = master.shape[1]
    scale = 1.0 / math.sqrt(lax.axis_size("dp") * lax.axis_size("seq") * g.shape[0])
    any_spec = pl.BlockSpec(memory_space=pl.ANY)
    vm = pltpu.VMEM
    act, new_master, new_moment, new_second, new_weight = pl.pallas_call(
        functools.partial(kernel, scale),
        out_shape=(
            jax.ShapeDtypeStruct((fine, features), BF16),
            jax.ShapeDtypeStruct((rows, width), F32),
            jax.ShapeDtypeStruct((rows, width), F32),
            jax.ShapeDtypeStruct((rows, width), F32),
            jax.ShapeDtypeStruct((2, 2, 2, rows // 4, width), BF16),
        ),
        in_specs=[any_spec] * 6,
        out_specs=[any_spec] * 5,
        scratch_shapes=[
            vm((512, 2048), BF16),
            vm((2, 2, 32, 64, 128), BF16),
            vm((8, 2, 32, 64, 128), BF16),
            vm((2, 2, 16, 64, 128), BF16),
            vm((2, 512, 1024), BF16),
            vm((2, 512, 1024), BF16),
            vm((2048, 1024), BF16),
            vm((2048, 1024), BF16),
            vm((2, 4, 128, 2048), BF16),
            vm((8, 128, 2048), BF16),
            vm((2, 128, 2048), BF16),
            vm((512, 2048), BF16),
            vm((2, 2, 4, 4, 64, 1024), BF16),
            vm((2, 2, 2, 2, 64, 1024), BF16),
            vm((2, 2, 2, 4, 64, 1024), BF16),
            vm((2, 2, 4, 64, 1024), BF16),
            vm((2, 2, 2, 32, 1024), BF16),
            vm((2, 2, 2, 64, 1024), BF16),
            vm((256, 1024), F32),
            vm((256, 1024), F32),
            vm((256, 1024), F32),
            vm((2, 2, 64, 1024), BF16),
            vm((4, 2048), F32),
            vm((4, 2048), F32),
            pltpu.SemaphoreType.DMA((COPIES,)),
            pltpu.SemaphoreType.DMA((COPIES,)),
            pltpu.SemaphoreType.DMA((LOCALS,)),
        ],
        compiler_params=pltpu.CompilerParams(
            collective_id=0, has_side_effects=True, vmem_limit_bytes=66_000_000
        ),
    )(x, g, w, master[0], moment[0], second[0])
    return (act[None], new_master[None], new_moment[None], new_second[None], new_weight.reshape(2, rows, width))


def solution(mesh):
    return jax.shard_map(
        per_device,
        mesh=mesh,
        in_specs=(
            P("dp", ("seq", "mp"), None),
            P("dp", "seq", "mp"),
            P("dp", None, "mp"),
            P("dp", "seq", "mp"),
            P("dp", "seq", "mp"),
            P("dp", "seq", "mp"),
        ),
        out_specs=(
            P("dp", ("seq", "mp"), None),
            P("dp", "seq", "mp"),
            P("dp", "seq", "mp"),
            P("dp", "seq", "mp"),
            P(None, "seq", "mp"),
        ),
        check_vma=False,
    )
```

```python
import functools
import math

import jax
import jax.numpy as jnp
from jax import lax
from jax.experimental import pallas as pl
from jax.experimental.pallas import tpu as pltpu
from jax.sharding import PartitionSpec as P

MESH = pl.DeviceIdType.MESH
SHORT = 4
SIDE = 4

first_beta = 0.9
second_beta = 0.95
first_fix = 1.0 - 0.9**10
second_fix = 1.0 - 0.95**10
adam_eps = 1e-08
learn_rate = 0.05
weight_decay = 0.1

COPIES = 80
LOCALS = 16

F32 = jnp.float32
BF16 = jnp.bfloat16


def kernel(
    scale, x_hbm, g_hbm, w_hbm, ma_hbm, mo_hbm, se_hbm,
    rbuf, brecv, ma, mo, se, nw,
    xf, xall, x2t, xrel, g2, g2s, wown, wsib, pbuf, actr, arel,
    dwp, r1, r2, st, r3, r4, bsend,
    send_sem, recv_sem, local_sem,
):
    d = lax.axis_index("dp")
    s = lax.axis_index("seq")
    m = lax.axis_index("mp")
    z, y = s // SIDE, s % SIDE
    h, c = m // 2, m % 2
    od, oh, oc = 1 - d, 1 - h, 1 - c

    def near(dd, hh, cc):
        return {"dp": dd, "mp": 2 * hh + cc}

    def slot(dd, hh, cc):
        return 4 * dd + 2 * hh + cc

    me = slot(d, h, c)
    sibling = near(d, h, oc)
    intra, intra_o = near(od, h, c), near(od, h, oc)
    inter, inter_o = near(od, oh, c), near(od, oh, oc)

    def at_seq(zz, yy):
        return {"seq": zz * SIDE + yy}

    up = lambda v: (v + 1) % SIDE
    down = lambda v: (v + SIDE - 1) % SIDE
    across = lambda v: (v + 2) % SIDE
    zp, zm = at_seq(up(z), y), at_seq(down(z), y)
    yp, ym = at_seq(z, up(y)), at_seq(z, down(y))
    total = 64
    place = s * 4 + m
    before = (place + total - 1) % total
    after = (place + 1) % total
    prev_dev = {"seq": before // 4, "mp": before % 4}
    next_dev = {"seq": after // 4, "mp": after % 4}

    sent, ids, local_ids = [], {}, {}

    def send(name, src, dst, device):
        i = ids.setdefault(name, len(ids))
        copy = pltpu.make_async_remote_copy(
            src_ref=src, dst_ref=dst, send_sem=send_sem.at[i], recv_sem=recv_sem.at[i],
            device_id=device, device_id_type=MESH,
        )
        copy.start()
        sent.append(copy)

    def arrived(name, dst):
        i = ids.setdefault(name, len(ids))
        pltpu.make_async_remote_copy(
            src_ref=dst, dst_ref=dst, send_sem=send_sem.at[i], recv_sem=recv_sem.at[i],
            device_id=sibling, device_id_type=MESH,
        ).wait_recv()

    def local(name, src, dst):
        copy = pltpu.make_async_copy(src, dst, local_sem.at[local_ids.setdefault(name, len(local_ids))])
        copy.start()
        return copy

    in_x = local("x", x_hbm, xf)
    in_g = local("g", g_hbm, g2.at[d])
    in_w = local("w", w_hbm.at[c], wown)
    in_ma = local("ma", ma_hbm, ma)
    in_mo = local("mo", mo_hbm, mo)
    in_se = local("se", se_hbm, se)

    barrier = pltpu.get_barrier_semaphore()
    partners = (sibling, intra, intra_o, inter, inter_o, zp, zm, yp, ym, prev_dev, next_dev)
    for device in partners:
        pl.semaphore_signal(barrier, inc=1, device_id=device, device_id_type=MESH)
    pl.semaphore_wait(barrier, len(partners))

    send("G0", g_hbm, g2.at[d], intra)
    send("G1", g_hbm, g2s.at[d], sibling)
    send("W", w_hbm.at[oc], wsib, sibling)

    in_x.wait()

    def turn(i, carry):
        p, tile = i // 4, i % 4
        rows = lax.broadcasted_iota(jnp.int32, (128, 512), 0)
        cols = lax.broadcasted_iota(jnp.int32, (128, 512), 1)
        pick = jnp.where(cols == 4 * rows + p, 1.0, 0.0).astype(BF16)
        got = jnp.dot(pick, xf[:, pl.ds(pl.multiple_of(tile * 512, 512), 512)], preferred_element_type=F32)
        turned = got.T.astype(BF16)
        for j in range(4):
            owner = (p % 2) * 8 + tile * 2 + j // 2
            where = owner if j % 2 == 0 else 16 + (owner % SIDE) * SIDE + owner // SIDE
            for ch in range(2):
                xall[p // 2, ch, where] = turned[j * 128 + ch * 64:j * 128 + ch * 64 + 64]
        return carry

    lax.fori_loop(0, 16, turn, 0)
    own_x = local("xown", xall.at[d], x2t.at[me])
    first, second = pl.ds(0, 16), pl.ds(16, 16)

    def start_x(ch):
        tag = str(ch)
        send("Xa" + tag, xall.at[d, ch, first], xrel.at[ch, 0], intra)
        send("Xb" + tag, xall.at[d, ch, second], xrel.at[ch, 1], inter)
        send("Xd" + tag, xall.at[od, ch], x2t.at[me, ch], inter)
        send("Xc" + tag, xall.at[od, ch], x2t.at[me, ch], intra)
        send("Xe" + tag, xall.at[d, ch], x2t.at[me, ch], sibling)

    def relay_b(ch):
        arrived("Xb" + str(ch), xrel.at[ch, 1])
        send("Xb2" + str(ch), xrel.at[ch, 1], x2t.at[slot(od, oh, c), ch, second], intra)

    def relay_a(ch):
        arrived("Xa" + str(ch), xrel.at[ch, 0])
        send("Xa2" + str(ch), xrel.at[ch, 0], x2t.at[slot(od, h, c), ch, first], inter)

    def pass_on(name, ch, dst):
        arrived(name + str(ch), dst)
        send("F" + name + str(ch), dst, dst, sibling)

    def passed(name, ch, dst):
        arrived("F" + name + str(ch), dst)

    def act_half(dd):
        def step(t, carry):
            outs = pl.ds(pl.multiple_of(t * 256, 256), 256)
            dims = (((1,), (1,)), ((), ()))
            part = lax.dot_general(g2[dd], wown[outs, :], dims, preferred_element_type=F32)
            part += lax.dot_general(g2s[dd], wsib[outs, :], dims, preferred_element_type=F32)
            pbuf[dd, :, :, outs] = part.astype(BF16).reshape(4, 128, 256)
            return carry

        lax.fori_loop(0, 8, step, 0)

    def grad_tile(ch, group_a, group_b):
        tile_a, tile_b = pl.ds(4 * group_a, 4), pl.ds(16 + 4 * group_b, 4)

        def step(t, carry):
            cols = pl.ds(pl.multiple_of(t * 256, 256), 256)
            left = jnp.concatenate(
                [
                    jnp.concatenate([x2t[k, ch, tile].reshape(256, 128) for k in range(8)], axis=1)
                    for tile in (tile_a, tile_b)
                ],
                axis=0,
            )
            right = jnp.concatenate([g2[0, :, cols], g2[1, :, cols]], axis=0)
            part = jnp.dot(left, right, preferred_element_type=F32).astype(BF16).reshape(2, 4, 64, 256)
            dwp[ch, 0, group_a, :, :, cols] = part[0]
            dwp[ch, 1, group_b, :, :, cols] = part[1]
            return carry

        lax.fori_loop(0, 4, step, 0)

    def wide(v):
        return v.astype(F32)

    halves = (("A", z, y, zp, zm, yp, ym), ("B", y, z, yp, ym, zp, zm))

    def reduce_1(ch):
        for i, (tag, a1, a2, p1, m1, p2, m2) in enumerate(halves):
            tag += str(ch)
            send(tag + "1p", dwp.at[ch, i, across(a1), pl.ds(0, 2)], r1.at[ch, i, 0], p1)
            send(tag + "1m", dwp.at[ch, i, across(a1), pl.ds(2, 2)], r1.at[ch, i, 1], m1)

    def reduce_2(ch):
        for i, (tag, a1, a2, p1, m1, p2, m2) in enumerate(halves):
            tag += str(ch)
            arrived(tag + "1p", r1.at[ch, i, 0])
            for j in range(2):
                dwp[ch, i, up(a1), j] = (wide(dwp[ch, i, up(a1), j]) + wide(r1[ch, i, 0, j])).astype(BF16)
            send(tag + "2p", dwp.at[ch, i, up(a1)], r2.at[ch, i, 0], p1)
            arrived(tag + "1m", r1.at[ch, i, 1])
            for j in range(2):
                dwp[ch, i, down(a1), 2 + j] = (
                    wide(dwp[ch, i, down(a1), 2 + j]) + wide(r1[ch, i, 1, j])
                ).astype(BF16)
            send(tag + "2m", dwp.at[ch, i, down(a1)], r2.at[ch, i, 1], m1)

    def reduce_3(ch):
        for i, (tag, a1, a2, p1, m1, p2, m2) in enumerate(halves):
            tag += str(ch)
            arrived(tag + "2p", r2.at[ch, i, 0])
            arrived(tag + "2m", r2.at[ch, i, 1])
            for j in range(4):
                st[ch, i, j] = (
                    wide(dwp[ch, i, a1, j]) + wide(r2[ch, i, 0, j]) + wide(r2[ch, i, 1, j])
                ).astype(BF16)
            send(tag + "3p", st.at[ch, i, across(a2), pl.ds(0, 32)], r3.at[ch, i, 0], p2)
            send(tag + "3m", st.at[ch, i, across(a2), pl.ds(32, 32)], r3.at[ch, i, 1], m2)

    def reduce_4(ch):
        for i, (tag, a1, a2, p1, m1, p2, m2) in enumerate(halves):
            tag += str(ch)
            arrived(tag + "3p", r3.at[ch, i, 0])
            st[ch, i, up(a2), 0:32] = (wide(st[ch, i, up(a2), 0:32]) + wide(r3[ch, i, 0])).astype(BF16)
            send(tag + "4p", st.at[ch, i, up(a2)], r4.at[ch, i, 0], p2)
            arrived(tag + "3m", r3.at[ch, i, 1])
            st[ch, i, down(a2), 32:64] = (
                wide(st[ch, i, down(a2), 32:64]) + wide(r3[ch, i, 1])
            ).astype(BF16)
            send(tag + "4m", st.at[ch, i, down(a2)], r4.at[ch, i, 1], m2)

    def update(ch):
        for i, (tag, a1, a2, p1, m1, p2, m2) in enumerate(halves):
            tag += str(ch)
            arrived(tag + "4p", r4.at[ch, i, 0])
            arrived(tag + "4m", r4.at[ch, i, 1])
            rows = slice(128 * i + 64 * ch, 128 * i + 64 * ch + 64)
            grad = (wide(st[ch, i, a2]) + wide(r4[ch, i, 0]) + wide(r4[ch, i, 1])) * scale
            new_moment = first_beta * mo[rows, :] + (1.0 - first_beta) * grad
            new_second = second_beta * se[rows, :] + (1.0 - second_beta) * grad * grad
            ratio = new_moment / first_fix / (jnp.sqrt(new_second / second_fix) + adam_eps)
            old = ma[rows, :]
            new_master = old - learn_rate * (ratio + weight_decay * old)
            mo[rows, :] = new_moment
            se[rows, :] = new_second
            ma[rows, :] = new_master
            nw[d, i, ch] = new_master.astype(BF16)
        both = pl.ds(0, 2)
        send("nw" + str(ch), nw.at[d, both, ch], nw.at[d, both, ch], intra)

    start_x(0)
    in_g.wait()
    in_w.wait()
    relay_b(0)
    start_x(1)
    arrived("G1", g2s.at[d])
    arrived("W", wsib)
    act_half(d)
    arrived("G0", g2.at[od])
    send("G2", g2.at[od], g2s.at[od], sibling)
    arrived("G2", g2s.at[od])
    act_half(od)
    relay_a(0)
    relay_b(1)

    send("Pd1", pbuf.at[d, 2 * oh + oc], arel.at[1], inter)
    send("Pd0", pbuf.at[d, 2 * oh + c], arel.at[0], intra)
    send("Pb0", pbuf.at[od, 2 * h + c], actr.at[me], intra)
    send("Pb1", pbuf.at[od, 2 * h + oc], actr.at[me], intra_o)
    send("Pa", pbuf.at[d, 2 * h + oc], actr.at[me], sibling)

    def pass_all(ch):
        pass_on("Xd", ch, x2t.at[slot(od, oh, c), ch])
        pass_on("Xc", ch, x2t.at[slot(od, h, c), ch])
        pass_on("Xa2", ch, x2t.at[slot(d, oh, c), ch, first])
        pass_on("Xb2", ch, x2t.at[slot(d, oh, c), ch, second])

    def all_passed(ch):
        arrived("Xe" + str(ch), x2t.at[slot(d, h, oc), ch])
        passed("Xd", ch, x2t.at[slot(od, oh, oc), ch])
        passed("Xc", ch, x2t.at[slot(od, h, oc), ch])
        passed("Xa2", ch, x2t.at[slot(d, oh, oc), ch, first])
        passed("Xb2", ch, x2t.at[slot(d, oh, oc), ch, second])

    pass_all(0)
    own_x.wait()
    all_passed(0)

    grad_tile(0, across(z), across(y))
    reduce_1(0)
    grad_tile(0, up(z), up(y))
    relay_a(1)
    send("Pc0", pbuf.at[od, 2 * oh + c], actr.at[me], inter)
    send("Pc1", pbuf.at[od, 2 * oh + oc], actr.at[me], inter_o)
    grad_tile(0, down(z), down(y))
    grad_tile(0, z, y)
    reduce_2(0)
    arrived("Pd1", arel.at[1])
    send("Pf1", arel.at[1], actr.at[slot(od, oh, c)], intra_o)

    pass_all(1)
    all_passed(1)
    grad_tile(1, across(z), across(y))
    reduce_1(1)
    reduce_3(0)
    grad_tile(1, up(z), up(y))
    grad_tile(1, down(z), down(y))
    reduce_4(0)
    grad_tile(1, z, y)
    reduce_2(1)
    arrived("Pd0", arel.at[0])
    send("Pf0", arel.at[0], actr.at[slot(od, h, c)], inter)
    in_ma.wait()
    in_mo.wait()
    in_se.wait()
    update(0)
    reduce_3(1)
    reduce_4(1)
    update(1)
    arrived("Pa", actr.at[slot(d, h, oc)])
    arrived("Pb0", actr.at[slot(od, h, c)])
    arrived("Pb1", actr.at[slot(od, h, oc)])
    arrived("Pc0", actr.at[slot(od, oh, c)])
    arrived("Pc1", actr.at[slot(od, oh, oc)])
    arrived("Pf0", actr.at[slot(d, oh, c)])
    arrived("Pf1", actr.at[slot(d, oh, oc)])
    actr[me] = pbuf[d, m]
    for p in range(4):
        k = 4 * (p // 2) + p % 2
        both = wide(actr[k]) + wide(actr[k + 2])
        rbuf[p * 128:(p + 1) * 128, :] = both.astype(BF16)
        bsend[p:p + 1, :] = both[0:1]
    send("bnd", bsend, brecv, prev_dev)
    arrived("bnd", brecv)
    for ch in range(2):
        arrived("nw" + str(ch), nw.at[od, pl.ds(0, 2), ch])
    for copy in sent:
        copy.wait_send()


def finish(r_ref, b_ref, ma, mo, se, nw, act_out, nm_out, nmo_out, ns_out, nw_out, act, act_sem, sem):
    copies = [
        pltpu.make_async_copy(src, dst, sem.at[i])
        for i, (src, dst) in enumerate(((ma, nm_out), (mo, nmo_out), (se, ns_out), (nw, nw_out)))
    ]
    for copy in copies:
        copy.start()
    last = lax.axis_index("seq") * 4 + lax.axis_index("mp") == 63
    rows = lax.broadcasted_iota(jnp.int32, (512, 512), 0)
    cols = lax.broadcasted_iota(jnp.int32, (512, 512), 1)
    put = jnp.where(rows == 4 * (cols % 128) + cols // 128 - 3, 1.0, 0.0).astype(BF16)
    line = lax.broadcasted_iota(jnp.int32, (16, 512), 0)
    for t in range(4):
        span = pl.ds(t * 512, 512)
        out = jnp.dot(put, r_ref[:, span], preferred_element_type=F32)
        act[0:496, span] = out[0:496].astype(BF16)
        tail = out[496:512]
        for p in range(3):
            row = jnp.where(last, 0.0, b_ref[p:p + 1, span])
            tail = jnp.where(line == 13 + p, row, tail)
        act[496:512, span] = tail.astype(BF16)
        copy = pltpu.make_async_copy(act.at[:, span], act_out.at[:, span], act_sem.at[t])
        copy.start()
        copies.append(copy)
    for copy in copies:
        copy.wait()


def per_device(shortening_input, coarse_grad, weight_copy, master, moment, second):
    x = shortening_input[0]
    g = coarse_grad[0]
    fine, features = x.shape
    width = g.shape[1]
    w = weight_copy.reshape(2, features, width)
    rows = master.shape[1]
    scale = 1.0 / math.sqrt(lax.axis_size("dp") * lax.axis_size("seq") * g.shape[0])
    any_spec = pl.BlockSpec(memory_space=pl.ANY)
    vm = pltpu.VMEM
    held = pl.pallas_call(
        functools.partial(kernel, scale),
        out_shape=(
            vm((fine, features), BF16),
            vm((4, features), F32),
            vm((rows, width), F32),
            vm((rows, width), F32),
            vm((rows, width), F32),
            vm((2, 2, 2, rows // 4, width), BF16),
        ),
        in_specs=[any_spec] * 6,
        out_specs=[pl.BlockSpec(memory_space=pltpu.VMEM)] * 6,
        scratch_shapes=[
            vm((512, 2048), BF16),
            vm((2, 2, 32, 64, 128), BF16),
            vm((8, 2, 32, 64, 128), BF16),
            vm((2, 2, 16, 64, 128), BF16),
            vm((2, 512, 1024), BF16),
            vm((2, 512, 1024), BF16),
            vm((2048, 1024), BF16),
            vm((2048, 1024), BF16),
            vm((2, 4, 128, 2048), BF16),
            vm((8, 128, 2048), BF16),
            vm((2, 128, 2048), BF16),
            vm((2, 2, 4, 4, 64, 1024), BF16),
            vm((2, 2, 2, 2, 64, 1024), BF16),
            vm((2, 2, 2, 4, 64, 1024), BF16),
            vm((2, 2, 4, 64, 1024), BF16),
            vm((2, 2, 2, 32, 1024), BF16),
            vm((2, 2, 2, 64, 1024), BF16),
            vm((4, 2048), F32),
            pltpu.SemaphoreType.DMA((COPIES,)),
            pltpu.SemaphoreType.DMA((COPIES,)),
            pltpu.SemaphoreType.DMA((LOCALS,)),
        ],
        compiler_params=pltpu.CompilerParams(
            collective_id=0, has_side_effects=True, vmem_limit_bytes=57_500_000
        ),
    )(x, g, w, master[0], moment[0], second[0])
    act, new_master, new_moment, new_second, new_weight = pl.pallas_call(
        finish,
        out_shape=(
            jax.ShapeDtypeStruct((fine, features), BF16),
            jax.ShapeDtypeStruct((rows, width), F32),
            jax.ShapeDtypeStruct((rows, width), F32),
            jax.ShapeDtypeStruct((rows, width), F32),
            jax.ShapeDtypeStruct((2, 2, 2, rows // 4, width), BF16),
        ),
        in_specs=[pl.BlockSpec(memory_space=pltpu.VMEM)] * 2 + [any_spec] * 4,
        out_specs=[any_spec] * 5,
        scratch_shapes=[
            vm((fine, features), BF16),
            pltpu.SemaphoreType.DMA((4,)),
            pltpu.SemaphoreType.DMA((4,)),
        ],
        compiler_params=pltpu.CompilerParams(vmem_limit_bytes=16_000_000),
    )(*held)
    return (act[None], new_master[None], new_moment[None], new_second[None], new_weight.reshape(2, rows, width))


def solution(mesh):
    return jax.shard_map(
        per_device,
        mesh=mesh,
        in_specs=(
            P("dp", ("seq", "mp"), None),
            P("dp", "seq", "mp"),
            P("dp", None, "mp"),
            P("dp", "seq", "mp"),
            P("dp", "seq", "mp"),
            P("dp", "seq", "mp"),
        ),
        out_specs=(
            P("dp", ("seq", "mp"), None),
            P("dp", "seq", "mp"),
            P("dp", "seq", "mp"),
            P("dp", "seq", "mp"),
            P(None, "seq", "mp"),
        ),
        check_vma=False,
    )
```

```python
import functools
import math

import jax
import jax.numpy as jnp
from jax import lax
from jax.experimental import pallas as pl
from jax.experimental.pallas import tpu as pltpu
from jax.sharding import PartitionSpec as P

MESH = pl.DeviceIdType.MESH
SHORT = 4
SIDE = 4

first_beta = 0.9
second_beta = 0.95
first_fix = 1.0 - 0.9**10
second_fix = 1.0 - 0.95**10
adam_eps = 1e-08
learn_rate = 0.05
weight_decay = 0.1

COPIES = 96
OWNED = 92
LOCALS = 16

F32 = jnp.float32
BF16 = jnp.bfloat16


def kernel(
    scale, x_hbm, g_hbm, w_hbm, ma_hbm, mo_hbm, se_hbm,
    rbuf, brecv, ma, mo, se, nw,
    xf, xall, x2t, xrel, gall, wown, wsib, pbuf, actr, arel,
    dwp, r1, r2, st, r3, r4, rsend, gr, bsend,
    send_sem, recv_sem, local_sem,
):
    d = lax.axis_index("dp")
    s = lax.axis_index("seq")
    m = lax.axis_index("mp")
    z, y = s // SIDE, s % SIDE
    h, c = m // 2, m % 2
    od, oh, oc = 1 - d, 1 - h, 1 - c

    def near(dd, hh, cc):
        return {"dp": dd, "mp": 2 * hh + cc}

    def slot(dd, hh, cc):
        return 4 * dd + 2 * hh + cc

    me = slot(d, h, c)
    sibling = near(d, h, oc)
    intra, intra_o = near(od, h, c), near(od, h, oc)
    inter, inter_o = near(od, oh, c), near(od, oh, oc)

    def at_seq(zz, yy):
        return {"seq": zz * SIDE + yy}

    up = lambda v: (v + 1) % SIDE
    down = lambda v: (v + SIDE - 1) % SIDE
    across = lambda v: (v + 2) % SIDE
    zp, zm = at_seq(up(z), y), at_seq(down(z), y)
    yp, ym = at_seq(z, up(y)), at_seq(z, down(y))
    total = 64
    place = s * 4 + m
    before = (place + total - 1) % total
    after = (place + 1) % total
    prev_dev = {"seq": before // 4, "mp": before % 4}
    next_dev = {"seq": after // 4, "mp": after % 4}

    sent, maybe, ids, local_ids = [], [], {}, {}

    def send(name, src, dst, device):
        i = ids.setdefault(name, len(ids))
        copy = pltpu.make_async_remote_copy(
            src_ref=src, dst_ref=dst, send_sem=send_sem.at[i], recv_sem=recv_sem.at[i],
            device_id=device, device_id_type=MESH,
        )
        copy.start()
        sent.append(copy)

    def arrived(name, dst):
        i = ids.setdefault(name, len(ids))
        pltpu.make_async_remote_copy(
            src_ref=dst, dst_ref=dst, send_sem=send_sem.at[i], recv_sem=recv_sem.at[i],
            device_id=sibling, device_id_type=MESH,
        ).wait_recv()

    def local(name, src, dst):
        copy = pltpu.make_async_copy(src, dst, local_sem.at[local_ids.setdefault(name, len(local_ids))])
        copy.start()
        return copy

    in_x = local("x", x_hbm, xf)
    in_g = local("g", g_hbm, gall.at[me])
    in_w = local("w", w_hbm.at[c], wown)
    in_ma = local("ma", ma_hbm, ma)
    in_mo = local("mo", mo_hbm, mo)
    in_se = local("se", se_hbm, se)

    barrier = pltpu.get_barrier_semaphore()
    partners = (sibling, intra, intra_o, inter, inter_o, zp, zm, yp, ym, prev_dev, next_dev)
    for device in partners:
        pl.semaphore_signal(barrier, inc=1, device_id=device, device_id_type=MESH)
    alone = z == m

    def owner_device(j):
        return {"seq": m * SIDE + y, "mp": j}

    def source_device(j):
        return {"seq": j * SIDE + y, "mp": z}

    for j in range(SIDE):
        for device in (owner_device(j), source_device(j)):
            pl.semaphore_signal(barrier, inc=1, device_id=device, device_id_type=MESH)
    pl.semaphore_wait(barrier, len(partners) + 2 * SIDE)

    send("Gi", g_hbm, gall.at[me], intra)
    send("Gx", g_hbm, gall.at[me], inter)
    send("Gs", g_hbm, gall.at[me], sibling)
    send("W", w_hbm.at[oc], wsib, sibling)

    in_x.wait()

    def turn(i, carry):
        p, tile = i // 4, i % 4
        rows = lax.broadcasted_iota(jnp.int32, (128, 512), 0)
        cols = lax.broadcasted_iota(jnp.int32, (128, 512), 1)
        pick = jnp.where(cols == 4 * rows + p, 1.0, 0.0).astype(BF16)
        got = jnp.dot(pick, xf[:, pl.ds(pl.multiple_of(tile * 512, 512), 512)], preferred_element_type=F32)
        turned = got.T.astype(BF16)
        for j in range(4):
            block = turned[j * 128:(j + 1) * 128].reshape(2, 64, 128)
            xall[p * 2 + tile // 2, (tile % 2) * 2 + j // 2, pl.ds((j % 2) * 2, 2)] = block
        return carry

    lax.fori_loop(0, 16, turn, 0)
    own_x = local("xown", xall.at[me], x2t.at[me])
    send("Xa", xall.at[slot(d, oh, c)], xrel.at[0], intra)
    send("Xb", xall.at[slot(d, oh, oc)], xrel.at[1], inter)
    send("Xi0", xall.at[slot(od, h, c)], x2t.at[me], intra)
    send("Xi1", xall.at[slot(od, h, oc)], x2t.at[me], intra_o)
    send("Xx0", xall.at[slot(od, oh, c)], x2t.at[me], inter)
    send("Xx1", xall.at[slot(od, oh, oc)], x2t.at[me], inter_o)
    send("Xs", xall.at[slot(d, h, oc)], x2t.at[me], sibling)

    def act_half(dd):
        def step(t, carry):
            outs = pl.ds(pl.multiple_of(t * 256, 256), 256)
            dims = (((1,), (1,)), ((), ()))
            part = lax.dot_general(gall[4 * dd + m], wown[outs, :], dims, preferred_element_type=F32)
            part += lax.dot_general(gall[4 * dd + 2 * h + oc], wsib[outs, :], dims, preferred_element_type=F32)
            pbuf[dd, :, :, outs] = part.astype(BF16).reshape(4, 128, 256)
            return carry

        lax.fori_loop(0, 8, step, 0)

    def grad_tile(ch, group_a, group_b):
        side = h if ch == 0 else oh

        def step(t, carry):
            cols = pl.ds(pl.multiple_of(t * 256, 256), 256)

            def product(rows, column):
                left = jnp.concatenate([rows(k).reshape(256, 128) for k in range(8)], axis=1)
                right = jnp.concatenate(
                    [gall[2 * side + column, :, cols], gall[4 + 2 * side + column, :, cols]], axis=0
                )
                part = jnp.dot(left, right, preferred_element_type=F32)
                return part.astype(BF16).reshape(4, 64, 256)

            dwp[ch, 0, group_a, :, :, cols] = product(lambda k: x2t[k, :, group_a], 0)
            dwp[ch, 1, group_b, :, :, cols] = product(lambda k: x2t[k, group_b], 1)
            return carry

        lax.fori_loop(0, 4, step, 0)

    def wide(v):
        return v.astype(F32)

    halves = (("A", z, y, zp, zm, yp, ym), ("B", y, z, yp, ym, zp, zm))

    def reduce_1(ch):
        for i, (tag, a1, a2, p1, m1, p2, m2) in enumerate(halves):
            tag += str(ch)
            send(tag + "1p", dwp.at[ch, i, across(a1), pl.ds(0, 2)], r1.at[ch, i, 0], p1)
            send(tag + "1m", dwp.at[ch, i, across(a1), pl.ds(2, 2)], r1.at[ch, i, 1], m1)

    def reduce_2(ch):
        for i, (tag, a1, a2, p1, m1, p2, m2) in enumerate(halves):
            tag += str(ch)
            arrived(tag + "1p", r1.at[ch, i, 0])
            for j in range(2):
                dwp[ch, i, up(a1), j] = (wide(dwp[ch, i, up(a1), j]) + wide(r1[ch, i, 0, j])).astype(BF16)
            send(tag + "2p", dwp.at[ch, i, up(a1)], r2.at[ch, i, 0], p1)
            arrived(tag + "1m", r1.at[ch, i, 1])
            for j in range(2):
                dwp[ch, i, down(a1), 2 + j] = (
                    wide(dwp[ch, i, down(a1), 2 + j]) + wide(r1[ch, i, 1, j])
                ).astype(BF16)
            send(tag + "2m", dwp.at[ch, i, down(a1)], r2.at[ch, i, 1], m1)

    def reduce_3(ch):
        for i, (tag, a1, a2, p1, m1, p2, m2) in enumerate(halves):
            tag += str(ch)
            arrived(tag + "2p", r2.at[ch, i, 0])
            arrived(tag + "2m", r2.at[ch, i, 1])
            for j in range(4):
                st[ch, i, j] = (
                    wide(dwp[ch, i, a1, j]) + wide(r2[ch, i, 0, j]) + wide(r2[ch, i, 1, j])
                ).astype(BF16)
            send(tag + "3p", st.at[ch, i, across(a2), pl.ds(0, 32)], r3.at[ch, i, 0], p2)
            send(tag + "3m", st.at[ch, i, across(a2), pl.ds(32, 32)], r3.at[ch, i, 1], m2)

    def reduce_4(ch):
        for i, (tag, a1, a2, p1, m1, p2, m2) in enumerate(halves):
            tag += str(ch)
            arrived(tag + "3p", r3.at[ch, i, 0])
            st[ch, i, up(a2), 0:32] = (wide(st[ch, i, up(a2), 0:32]) + wide(r3[ch, i, 0])).astype(BF16)
            send(tag + "4p", st.at[ch, i, up(a2)], r4.at[ch, i, 0], p2)
            arrived(tag + "3m", r3.at[ch, i, 1])
            st[ch, i, down(a2), 32:64] = (
                wide(st[ch, i, down(a2), 32:64]) + wide(r3[ch, i, 1])
            ).astype(BF16)
            send(tag + "4m", st.at[ch, i, down(a2)], r4.at[ch, i, 1], m2)

    def hand_over(ch):
        for i, (tag, a1, a2, p1, m1, p2, m2) in enumerate(halves):
            tag += str(ch)
            arrived(tag + "4p", r4.at[ch, i, 0])
            arrived(tag + "4m", r4.at[ch, i, 1])
            rsend[ch, i] = (wide(st[ch, i, a2]) + wide(r4[ch, i, 0]) + wide(r4[ch, i, 1])).astype(BF16)
            column = 2 * (h if ch == 0 else oh) + i
            k = ids.setdefault("R" + tag, len(ids))
            copy = pltpu.make_async_remote_copy(
                src_ref=rsend.at[ch, i], dst_ref=gr.at[z], send_sem=send_sem.at[k], recv_sem=recv_sem.at[OWNED + z],
                device_id=owner_device(column), device_id_type=MESH,
            )
            if ch == 1:
                copy.start()
                sent.append(copy)
                continue
            mine = alone & (c == i)
            maybe.append((mine, copy))

            @pl.when(jnp.logical_not(mine))
            def _():
                copy.start()

            @pl.when(mine)
            def _():
                pltpu.make_async_copy(rsend.at[ch, i], gr.at[z], recv_sem.at[OWNED + z]).start()

    def update():
        for j in range(SIDE):
            pltpu.make_async_remote_copy(
                src_ref=gr.at[j], dst_ref=gr.at[j], send_sem=send_sem.at[OWNED + j], recv_sem=recv_sem.at[OWNED + j],
                device_id=sibling, device_id_type=MESH,
            ).wait_recv()
            rows = slice(64 * j, 64 * j + 64)
            grad = wide(gr[j]) * scale
            new_moment = first_beta * mo[rows, :] + (1.0 - first_beta) * grad
            new_second = second_beta * se[rows, :] + (1.0 - second_beta) * grad * grad
            ratio = new_moment / first_fix / (jnp.sqrt(new_second / second_fix) + adam_eps)
            old = ma[rows, :]
            new_master = old - learn_rate * (ratio + weight_decay * old)
            mo[rows, :] = new_moment
            se[rows, :] = new_second
            ma[rows, :] = new_master
            nw[d, rows, :] = new_master.astype(BF16)
            if j % 2 == 1:
                both = pl.ds(64 * j - 64, 128)
                send("nw" + str(j // 2), nw.at[d, both], nw.at[d, both], intra)

    def pass_on(name, came, dst):
        arrived(came, dst)
        send(name, dst, dst, sibling)

    in_g.wait()
    in_w.wait()
    arrived("Gs", gall.at[slot(d, h, oc)])
    arrived("W", wsib)
    act_half(d)
    pass_on("Fi", "Gi", gall.at[slot(od, h, c)])
    pass_on("Fx", "Gx", gall.at[slot(od, oh, c)])
    arrived("Xa", xrel.at[0])
    send("Xa2", xrel.at[0], x2t.at[slot(od, h, c)], inter)
    arrived("Xb", xrel.at[1])
    send("Xb2", xrel.at[1], x2t.at[slot(od, oh, c)], intra_o)
    most, rest = pl.ds(0, 384), pl.ds(384, 128)
    send("Ga", gall.at[slot(od, h, c), most], gall.at[slot(od, h, c), most], inter)
    send("Gb", gall.at[slot(od, oh, c), rest], gall.at[slot(od, oh, c), rest], intra)
    arrived("Fi", gall.at[slot(od, h, oc)])
    act_half(od)

    send("Pd1", pbuf.at[d, 2 * oh + oc], arel.at[1], inter)
    send("Pd0", pbuf.at[d, 2 * oh + c], arel.at[0], intra)
    send("Pb0", pbuf.at[od, 2 * h + c], actr.at[me], intra)
    send("Pb1", pbuf.at[od, 2 * h + oc], actr.at[me], intra_o)
    send("Pc0", pbuf.at[od, 2 * oh + c], actr.at[me], inter)
    send("Pc1", pbuf.at[od, 2 * oh + oc], actr.at[me], inter_o)
    send("Pa", pbuf.at[d, 2 * h + oc], actr.at[me], sibling)

    own_x.wait()
    arrived("Xs", x2t.at[slot(d, h, oc)])
    arrived("Xi0", x2t.at[slot(od, h, c)])
    arrived("Xi1", x2t.at[slot(od, h, oc)])
    arrived("Xx0", x2t.at[slot(od, oh, c)])
    arrived("Xx1", x2t.at[slot(od, oh, oc)])
    arrived("Xa2", x2t.at[slot(d, oh, c)])
    arrived("Xb2", x2t.at[slot(d, oh, oc)])

    grad_tile(0, across(z), across(y))
    reduce_1(0)
    grad_tile(0, up(z), up(y))
    grad_tile(0, down(z), down(y))
    pass_on("Fb", "Gb", gall.at[slot(d, oh, c), rest])
    grad_tile(0, z, y)
    reduce_2(0)
    pass_on("Fa", "Ga", gall.at[slot(d, oh, c), most])
    arrived("Fx", gall.at[slot(od, oh, oc)])
    arrived("Fb", gall.at[slot(d, oh, oc), rest])
    arrived("Fa", gall.at[slot(d, oh, oc), most])
    grad_tile(1, across(z), across(y))
    reduce_1(1)
    reduce_3(0)
    grad_tile(1, up(z), up(y))
    grad_tile(1, down(z), down(y))
    reduce_4(0)
    grad_tile(1, z, y)
    arrived("Pd0", arel.at[0])
    send("Pf0", arel.at[0], actr.at[slot(od, h, c)], inter)
    reduce_2(1)
    arrived("Pd1", arel.at[1])
    send("Pf1", arel.at[1], actr.at[slot(od, oh, c)], intra_o)
    hand_over(0)
    in_ma.wait()
    in_mo.wait()
    in_se.wait()
    reduce_3(1)
    reduce_4(1)
    hand_over(1)
    update()

    arrived("Pa", actr.at[slot(d, h, oc)])
    arrived("Pb0", actr.at[slot(od, h, c)])
    arrived("Pb1", actr.at[slot(od, h, oc)])
    arrived("Pc0", actr.at[slot(od, oh, c)])
    arrived("Pc1", actr.at[slot(od, oh, oc)])
    arrived("Pf0", actr.at[slot(d, oh, c)])
    arrived("Pf1", actr.at[slot(d, oh, oc)])
    actr[me] = pbuf[d, m]
    for p in range(4):
        k = 4 * (p // 2) + p % 2
        both = wide(actr[k]) + wide(actr[k + 2])
        rbuf[p * 128:(p + 1) * 128, :] = both.astype(BF16)
        bsend[p:p + 1, :] = both[0:1]
    send("bnd", bsend, brecv, prev_dev)
    arrived("bnd", brecv)
    for j in range(2):
        arrived("nw" + str(j), nw.at[od, pl.ds(128 * j, 128)])
    for mine, copy in maybe:

        @pl.when(jnp.logical_not(mine))
        def _():
            copy.wait_send()

    for copy in sent:
        copy.wait_send()


def finish(r_ref, b_ref, ma, mo, se, nw, act_out, nm_out, nmo_out, ns_out, nw_out, act, act_sem, sem):
    copies = [
        pltpu.make_async_copy(src, dst, sem.at[i])
        for i, (src, dst) in enumerate(((ma, nm_out), (mo, nmo_out), (se, ns_out), (nw, nw_out)))
    ]
    for copy in copies:
        copy.start()
    last = lax.axis_index("seq") * 4 + lax.axis_index("mp") == 63
    rows = lax.broadcasted_iota(jnp.int32, (512, 512), 0)
    cols = lax.broadcasted_iota(jnp.int32, (512, 512), 1)
    put = jnp.where(rows == 4 * (cols % 128) + cols // 128 - 3, 1.0, 0.0).astype(BF16)
    line = lax.broadcasted_iota(jnp.int32, (16, 512), 0)
    for t in range(4):
        span = pl.ds(t * 512, 512)
        out = jnp.dot(put, r_ref[:, span], preferred_element_type=F32)
        act[0:496, span] = out[0:496].astype(BF16)
        tail = out[496:512]
        for p in range(3):
            row = jnp.where(last, 0.0, b_ref[p:p + 1, span])
            tail = jnp.where(line == 13 + p, row, tail)
        act[496:512, span] = tail.astype(BF16)
        copy = pltpu.make_async_copy(act.at[:, span], act_out.at[:, span], act_sem.at[t])
        copy.start()
        copies.append(copy)
    for copy in copies:
        copy.wait()


def per_device(shortening_input, coarse_grad, weight_copy, master, moment, second):
    x = shortening_input[0]
    g = coarse_grad[0]
    fine, features = x.shape
    width = g.shape[1]
    w = weight_copy.reshape(2, features, width)
    rows = master.shape[1]
    scale = 1.0 / math.sqrt(lax.axis_size("dp") * lax.axis_size("seq") * g.shape[0])
    any_spec = pl.BlockSpec(memory_space=pl.ANY)
    vm = pltpu.VMEM
    held = pl.pallas_call(
        functools.partial(kernel, scale),
        out_shape=(
            vm((fine, features), BF16),
            vm((4, features), F32),
            vm((rows, width), F32),
            vm((rows, width), F32),
            vm((rows, width), F32),
            vm((2, rows, width), BF16),
        ),
        in_specs=[any_spec] * 6,
        out_specs=[pl.BlockSpec(memory_space=pltpu.VMEM)] * 6,
        scratch_shapes=[
            vm((512, 2048), BF16),
            vm((8, 4, 4, 64, 128), BF16),
            vm((8, 4, 4, 64, 128), BF16),
            vm((2, 4, 4, 64, 128), BF16),
            vm((8, 512, 1024), BF16),
            vm((2048, 1024), BF16),
            vm((2048, 1024), BF16),
            vm((2, 4, 128, 2048), BF16),
            vm((8, 128, 2048), BF16),
            vm((2, 128, 2048), BF16),
            vm((2, 2, 4, 4, 64, 1024), BF16),
            vm((2, 2, 2, 2, 64, 1024), BF16),
            vm((2, 2, 2, 4, 64, 1024), BF16),
            vm((2, 2, 4, 64, 1024), BF16),
            vm((2, 2, 2, 32, 1024), BF16),
            vm((2, 2, 2, 64, 1024), BF16),
            vm((2, 2, 64, 1024), BF16),
            vm((4, 64, 1024), BF16),
            vm((4, 2048), F32),
            pltpu.SemaphoreType.DMA((COPIES,)),
            pltpu.SemaphoreType.DMA((COPIES,)),
            pltpu.SemaphoreType.DMA((LOCALS,)),
        ],
        compiler_params=pltpu.CompilerParams(
            collective_id=0, has_side_effects=True, vmem_limit_bytes=57_500_000
        ),
    )(x, g, w, master[0], moment[0], second[0])
    act, new_master, new_moment, new_second, new_weight = pl.pallas_call(
        finish,
        out_shape=(
            jax.ShapeDtypeStruct((fine, features), BF16),
            jax.ShapeDtypeStruct((rows, width), F32),
            jax.ShapeDtypeStruct((rows, width), F32),
            jax.ShapeDtypeStruct((rows, width), F32),
            jax.ShapeDtypeStruct((2, rows, width), BF16),
        ),
        in_specs=[pl.BlockSpec(memory_space=pltpu.VMEM)] * 2 + [any_spec] * 4,
        out_specs=[any_spec] * 5,
        scratch_shapes=[
            vm((fine, features), BF16),
            pltpu.SemaphoreType.DMA((4,)),
            pltpu.SemaphoreType.DMA((4,)),
        ],
        compiler_params=pltpu.CompilerParams(vmem_limit_bytes=16_000_000),
    )(*held)
    return (act[None], new_master[None], new_moment[None], new_second[None], new_weight)


def solution(mesh):
    return jax.shard_map(
        per_device,
        mesh=mesh,
        in_specs=(
            P("dp", ("seq", "mp"), None),
            P("dp", "seq", "mp"),
            P("dp", None, "mp"),
            P("dp", "seq", "mp"),
            P("dp", "seq", "mp"),
            P("dp", "seq", "mp"),
        ),
        out_specs=(
            P("dp", ("seq", "mp"), None),
            P("dp", "seq", "mp"),
            P("dp", "seq", "mp"),
            P("dp", "seq", "mp"),
            P(None, "seq", "mp"),
        ),
        check_vma=False,
    )
```

```python
import functools
import math

import jax
import jax.numpy as jnp
from jax import lax
from jax.experimental import pallas as pl
from jax.experimental.pallas import tpu as pltpu
from jax.sharding import PartitionSpec as P

MESH = pl.DeviceIdType.MESH
SHORT = 4
SIDE = 4

first_beta = 0.9
second_beta = 0.95
first_fix = 1.0 - 0.9**10
second_fix = 1.0 - 0.95**10
adam_eps = 1e-08
learn_rate = 0.05
weight_decay = 0.1

COPIES = 160
OWNED = 152
LOCALS = 16

F32 = jnp.float32
BF16 = jnp.bfloat16


def kernel(
    scale, x_hbm, g_hbm, w_hbm, ma_hbm, mo_hbm, se_hbm,
    rbuf, brecv, ma, mo, se, nw,
    xf, xall, x2t, xrel, gall, wown, wsib, pbuf, actr, arel,
    dwp, r1, r2, st, r3, r4, rsend, gr, bsend,
    send_sem, recv_sem, local_sem,
):
    d = lax.axis_index("dp")
    s = lax.axis_index("seq")
    m = lax.axis_index("mp")
    z, y = s // SIDE, s % SIDE
    h, c = m // 2, m % 2
    od, oh, oc = 1 - d, 1 - h, 1 - c

    def near(dd, hh, cc):
        return {"dp": dd, "mp": 2 * hh + cc}

    def slot(dd, hh, cc):
        return 4 * dd + 2 * hh + cc

    me = slot(d, h, c)
    sibling = near(d, h, oc)
    intra, intra_o = near(od, h, c), near(od, h, oc)
    inter, inter_o = near(od, oh, c), near(od, oh, oc)

    def at_seq(zz, yy):
        return {"seq": zz * SIDE + yy}

    up = lambda v: (v + 1) % SIDE
    down = lambda v: (v + SIDE - 1) % SIDE
    across = lambda v: (v + 2) % SIDE
    zp, zm = at_seq(up(z), y), at_seq(down(z), y)
    yp, ym = at_seq(z, up(y)), at_seq(z, down(y))
    total = 64
    place = s * 4 + m
    before = (place + total - 1) % total
    after = (place + 1) % total
    prev_dev = {"seq": before // 4, "mp": before % 4}
    next_dev = {"seq": after // 4, "mp": after % 4}

    sent, maybe, ids, local_ids = [], [], {}, {}

    def send(name, src, dst, device):
        i = ids.setdefault(name, len(ids))
        copy = pltpu.make_async_remote_copy(
            src_ref=src, dst_ref=dst, send_sem=send_sem.at[i], recv_sem=recv_sem.at[i],
            device_id=device, device_id_type=MESH,
        )
        copy.start()
        sent.append(copy)

    def arrived(name, dst):
        i = ids.setdefault(name, len(ids))
        pltpu.make_async_remote_copy(
            src_ref=dst, dst_ref=dst, send_sem=send_sem.at[i], recv_sem=recv_sem.at[i],
            device_id=sibling, device_id_type=MESH,
        ).wait_recv()

    def local(name, src, dst):
        copy = pltpu.make_async_copy(src, dst, local_sem.at[local_ids.setdefault(name, len(local_ids))])
        copy.start()
        return copy

    in_x = local("x", x_hbm, xf)
    in_g = local("g", g_hbm, gall.at[me])
    in_w = local("w", w_hbm.at[c], wown)
    in_ma = local("ma", ma_hbm, ma)
    in_mo = local("mo", mo_hbm, mo)
    in_se = local("se", se_hbm, se)

    barrier = pltpu.get_barrier_semaphore()
    partners = (sibling, intra, intra_o, inter, inter_o, zp, zm, yp, ym, prev_dev, next_dev)
    for device in partners:
        pl.semaphore_signal(barrier, inc=1, device_id=device, device_id_type=MESH)
    alone = z == m

    def owner_device(j):
        return {"seq": m * SIDE + y, "mp": j}

    def source_device(j):
        return {"seq": j * SIDE + y, "mp": z}

    for j in range(SIDE):
        for device in (owner_device(j), source_device(j)):
            pl.semaphore_signal(barrier, inc=1, device_id=device, device_id_type=MESH)
    pl.semaphore_wait(barrier, len(partners) + 2 * SIDE)

    span = (pl.ds(0, 512), pl.ds(512, 512))

    def send_g(name, half, device):
        send(name, g_hbm.at[:, span[half]], gall.at[me, :, span[half]], device)

    send_g("Gi0", 0, intra)
    send("Gs", g_hbm, gall.at[me], sibling)
    send("W", w_hbm.at[oc], wsib, sibling)

    in_x.wait()

    def turn(i, carry):
        p, tile = i // 4, i % 4
        rows = lax.broadcasted_iota(jnp.int32, (128, 512), 0)
        cols = lax.broadcasted_iota(jnp.int32, (128, 512), 1)
        pick = jnp.where(cols == 4 * rows + p, 1.0, 0.0).astype(BF16)
        got = jnp.dot(pick, xf[:, pl.ds(pl.multiple_of(tile * 512, 512), 512)], preferred_element_type=F32)
        turned = got.T.astype(BF16)
        for j in range(4):
            block = turned[j * 128:(j + 1) * 128].reshape(2, 64, 128)
            xall[p * 2 + tile // 2, (tile % 2) * 2 + j // 2, pl.ds((j % 2) * 2, 2)] = block
        return carry

    lax.fori_loop(0, 16, turn, 0)
    own_x = local("xown", xall.at[me], x2t.at[me])
    send("Xb", xall.at[slot(d, oh, oc)], xrel.at[1], inter)
    send("Xa", xall.at[slot(d, oh, c)], xrel.at[0], intra)
    send("Xi0", xall.at[slot(od, h, c)], x2t.at[me], intra)
    send("Xi1", xall.at[slot(od, h, oc)], x2t.at[me], intra_o)
    send("Xx0", xall.at[slot(od, oh, c)], x2t.at[me], inter)
    send("Xx1", xall.at[slot(od, oh, oc)], x2t.at[me], inter_o)
    send("Xs", xall.at[slot(d, h, oc)], x2t.at[me], sibling)

    def act_part(dd, start, stop):
        def step(t, carry):
            outs = pl.ds(pl.multiple_of(t * 256, 256), 256)
            dims = (((1,), (1,)), ((), ()))
            part = lax.dot_general(gall[4 * dd + m], wown[outs, :], dims, preferred_element_type=F32)
            part += lax.dot_general(gall[4 * dd + 2 * h + oc], wsib[outs, :], dims, preferred_element_type=F32)
            pbuf[dd, :, :, outs] = part.astype(BF16).reshape(4, 128, 256)
            return carry

        lax.fori_loop(start, stop, step, 0)

    def grad_tile(ch, group_a, group_b):
        side = h if ch < 2 else oh

        def step(t, carry):
            cols = pl.ds(pl.multiple_of(t * 256, 256), 256)
            wide_cols = pl.ds(pl.multiple_of(ch % 2 * 512 + t * 256, 256), 256)

            def product(rows, column):
                left = jnp.concatenate([rows(k).reshape(256, 128) for k in range(8)], axis=1)
                right = jnp.concatenate(
                    [gall[2 * side + column, :, wide_cols], gall[4 + 2 * side + column, :, wide_cols]], axis=0
                )
                part = jnp.dot(left, right, preferred_element_type=F32)
                return part.astype(BF16).reshape(4, 64, 256)

            dwp[ch, 0, group_a, :, :, cols] = product(lambda k: x2t[k, :, group_a], 0)
            dwp[ch, 1, group_b, :, :, cols] = product(lambda k: x2t[k, group_b], 1)
            return carry

        lax.fori_loop(0, 2, step, 0)

    def wide(v):
        return v.astype(F32)

    halves = (("A", z, y, zp, zm, yp, ym), ("B", y, z, yp, ym, zp, zm))

    def reduce_1(ch):
        for i, (tag, a1, a2, p1, m1, p2, m2) in enumerate(halves):
            tag += str(ch)
            send(tag + "1p", dwp.at[ch, i, across(a1), pl.ds(0, 2)], r1.at[ch, i, 0], p1)
            send(tag + "1m", dwp.at[ch, i, across(a1), pl.ds(2, 2)], r1.at[ch, i, 1], m1)

    def reduce_2(ch):
        for i, (tag, a1, a2, p1, m1, p2, m2) in enumerate(halves):
            tag += str(ch)
            arrived(tag + "1p", r1.at[ch, i, 0])
            for j in range(2):
                dwp[ch, i, up(a1), j] = (wide(dwp[ch, i, up(a1), j]) + wide(r1[ch, i, 0, j])).astype(BF16)
            send(tag + "2p", dwp.at[ch, i, up(a1)], r2.at[ch, i, 0], p1)
            arrived(tag + "1m", r1.at[ch, i, 1])
            for j in range(2):
                dwp[ch, i, down(a1), 2 + j] = (
                    wide(dwp[ch, i, down(a1), 2 + j]) + wide(r1[ch, i, 1, j])
                ).astype(BF16)
            send(tag + "2m", dwp.at[ch, i, down(a1)], r2.at[ch, i, 1], m1)

    def reduce_3(ch):
        for i, (tag, a1, a2, p1, m1, p2, m2) in enumerate(halves):
            tag += str(ch)
            arrived(tag + "2p", r2.at[ch, i, 0])
            arrived(tag + "2m", r2.at[ch, i, 1])
            for j in range(4):
                st[ch, i, j] = (
                    wide(dwp[ch, i, a1, j]) + wide(r2[ch, i, 0, j]) + wide(r2[ch, i, 1, j])
                ).astype(BF16)
            send(tag + "3p", st.at[ch, i, across(a2), pl.ds(0, 32)], r3.at[ch, i, 0], p2)
            send(tag + "3m", st.at[ch, i, across(a2), pl.ds(32, 32)], r3.at[ch, i, 1], m2)

    def reduce_4(ch):
        for i, (tag, a1, a2, p1, m1, p2, m2) in enumerate(halves):
            tag += str(ch)
            arrived(tag + "3p", r3.at[ch, i, 0])
            st[ch, i, up(a2), 0:32] = (wide(st[ch, i, up(a2), 0:32]) + wide(r3[ch, i, 0])).astype(BF16)
            send(tag + "4p", st.at[ch, i, up(a2)], r4.at[ch, i, 0], p2)
            arrived(tag + "3m", r3.at[ch, i, 1])
            st[ch, i, down(a2), 32:64] = (
                wide(st[ch, i, down(a2), 32:64]) + wide(r3[ch, i, 1])
            ).astype(BF16)
            send(tag + "4m", st.at[ch, i, down(a2)], r4.at[ch, i, 1], m2)

    def hand_over(ch):
        for i, (tag, a1, a2, p1, m1, p2, m2) in enumerate(halves):
            tag += str(ch)
            arrived(tag + "4p", r4.at[ch, i, 0])
            arrived(tag + "4m", r4.at[ch, i, 1])
            rsend[ch, i] = (wide(st[ch, i, a2]) + wide(r4[ch, i, 0]) + wide(r4[ch, i, 1])).astype(BF16)
            column = 2 * (h if ch < 2 else oh) + i
            mark = OWNED + 2 * z + ch % 2
            home = gr.at[z, ch % 2]
            k = ids.setdefault("R" + tag, len(ids))
            copy = pltpu.make_async_remote_copy(
                src_ref=rsend.at[ch, i], dst_ref=home, send_sem=send_sem.at[k], recv_sem=recv_sem.at[mark],
                device_id=owner_device(column), device_id_type=MESH,
            )
            if ch >= 2:
                copy.start()
                sent.append(copy)
                continue
            mine = alone & (c == i)
            maybe.append((mine, copy))

            @pl.when(jnp.logical_not(mine))
            def _():
                copy.start()

            @pl.when(mine)
            def _():
                pltpu.make_async_copy(rsend.at[ch, i], home, recv_sem.at[mark]).start()

    def update():
        for j in range(SIDE):
            rows = slice(64 * j, 64 * j + 64)
            for half in range(2):
                mark = OWNED + 2 * j + half
                pltpu.make_async_remote_copy(
                    src_ref=gr.at[j, half], dst_ref=gr.at[j, half], send_sem=send_sem.at[mark],
                    recv_sem=recv_sem.at[mark], device_id=sibling, device_id_type=MESH,
                ).wait_recv()
                cols = slice(512 * half, 512 * half + 512)
                grad = wide(gr[j, half]) * scale
                new_moment = first_beta * mo[rows, cols] + (1.0 - first_beta) * grad
                new_second = second_beta * se[rows, cols] + (1.0 - second_beta) * grad * grad
                ratio = new_moment / first_fix / (jnp.sqrt(new_second / second_fix) + adam_eps)
                old = ma[rows, cols]
                new_master = old - learn_rate * (ratio + weight_decay * old)
                mo[rows, cols] = new_moment
                se[rows, cols] = new_second
                ma[rows, cols] = new_master
                nw[d, rows, cols] = new_master.astype(BF16)
            if j % 2 == 1:
                both = pl.ds(64 * j - 64, 128)
                send("nw" + str(j // 2), nw.at[d, both], nw.at[d, both], intra)

    def pass_on(name, came, dst):
        arrived(came, dst)
        send(name, dst, dst, sibling)

    def piece(k, half):
        return gall.at[k, :, span[half]]

    def tiles(ch):
        grad_tile(ch, across(z), across(y))
        reduce_1(ch)
        grad_tile(ch, up(z), up(y))
        grad_tile(ch, down(z), down(y))
        grad_tile(ch, z, y)

    arrived("Xb", xrel.at[1])
    send("Xb2", xrel.at[1], x2t.at[slot(od, oh, c)], intra_o)
    send_g("Gi1", 1, intra)
    in_g.wait()
    in_w.wait()
    arrived("Gs", gall.at[slot(d, h, oc)])
    arrived("W", wsib)
    act_part(d, 0, 8)
    arrived("Xa", xrel.at[0])
    send("Xa2", xrel.at[0], x2t.at[slot(od, h, c)], inter)
    send_g("Gx1", 1, inter)
    send_g("Gx0", 0, inter)
    pass_on("Fi0", "Gi0", piece(slot(od, h, c), 0))
    send("Ga", piece(slot(od, h, c), 0), piece(slot(od, h, c), 0), inter)

    own_x.wait()
    arrived("Xs", x2t.at[slot(d, h, oc)])
    arrived("Xi0", x2t.at[slot(od, h, c)])
    arrived("Xi1", x2t.at[slot(od, h, oc)])
    arrived("Xx0", x2t.at[slot(od, oh, c)])
    arrived("Xx1", x2t.at[slot(od, oh, oc)])
    arrived("Xa2", x2t.at[slot(d, oh, c)])
    arrived("Xb2", x2t.at[slot(d, oh, oc)])
    arrived("Fi0", piece(slot(od, h, oc), 0))
    tiles(0)
    pass_on("Fx1", "Gx1", piece(slot(od, oh, c), 1))
    send("Gb", piece(slot(od, oh, c), 1), piece(slot(od, oh, c), 1), intra)
    reduce_2(0)
    send("Pd1", pbuf.at[d, 2 * oh + oc], arel.at[1], inter)
    send("Pd0", pbuf.at[d, 2 * oh + c], arel.at[0], intra)
    send("Pa", pbuf.at[d, 2 * h + oc], actr.at[me], sibling)

    pass_on("Fi1", "Gi1", piece(slot(od, h, c), 1))
    arrived("Fi1", piece(slot(od, h, oc), 1))
    tiles(1)
    reduce_3(0)
    act_part(od, 0, 2)
    reduce_2(1)
    pass_on("Fx0", "Gx0", piece(slot(od, oh, c), 0))
    act_part(od, 2, 4)
    reduce_4(0)
    act_part(od, 4, 6)
    pass_on("Fb", "Gb", piece(slot(d, oh, c), 1))
    act_part(od, 6, 8)
    send("Pb0", pbuf.at[od, 2 * h + c], actr.at[me], intra)
    send("Pb1", pbuf.at[od, 2 * h + oc], actr.at[me], intra_o)
    send("Pc0", pbuf.at[od, 2 * oh + c], actr.at[me], inter)
    send("Pc1", pbuf.at[od, 2 * oh + oc], actr.at[me], inter_o)
    pass_on("Fa", "Ga", piece(slot(d, oh, c), 0))
    arrived("Fx1", piece(slot(od, oh, oc), 1))
    arrived("Fb", piece(slot(d, oh, oc), 1))
    tiles(3)
    arrived("Fx0", piece(slot(od, oh, oc), 0))
    arrived("Fa", piece(slot(d, oh, oc), 0))
    grad_tile(2, across(z), across(y))
    reduce_1(2)
    reduce_3(1)
    reduce_2(3)
    grad_tile(2, up(z), up(y))
    grad_tile(2, down(z), down(y))
    grad_tile(2, z, y)
    reduce_2(2)
    reduce_4(1)
    arrived("Pd0", arel.at[0])
    send("Pf0", arel.at[0], actr.at[slot(od, h, c)], inter)
    hand_over(0)
    arrived("Pd1", arel.at[1])
    send("Pf1", arel.at[1], actr.at[slot(od, oh, c)], intra_o)
    reduce_3(3)
    hand_over(1)
    reduce_3(2)
    reduce_4(3)
    reduce_4(2)
    hand_over(3)
    hand_over(2)
    in_ma.wait()
    in_mo.wait()
    in_se.wait()
    update()

    arrived("Pa", actr.at[slot(d, h, oc)])
    arrived("Pb0", actr.at[slot(od, h, c)])
    arrived("Pb1", actr.at[slot(od, h, oc)])
    arrived("Pc0", actr.at[slot(od, oh, c)])
    arrived("Pc1", actr.at[slot(od, oh, oc)])
    arrived("Pf0", actr.at[slot(d, oh, c)])
    arrived("Pf1", actr.at[slot(d, oh, oc)])
    actr[me] = pbuf[d, m]
    for p in range(4):
        k = 4 * (p // 2) + p % 2
        both = wide(actr[k]) + wide(actr[k + 2])
        rbuf[p * 128:(p + 1) * 128, :] = both.astype(BF16)
        bsend[p:p + 1, :] = both[0:1]
    send("bnd", bsend, brecv, prev_dev)
    arrived("bnd", brecv)
    for j in range(2):
        arrived("nw" + str(j), nw.at[od, pl.ds(128 * j, 128)])
    for mine, copy in maybe:

        @pl.when(jnp.logical_not(mine))
        def _():
            copy.wait_send()

    for copy in sent:
        copy.wait_send()


def finish(r_ref, b_ref, ma, mo, se, nw, act_out, nm_out, nmo_out, ns_out, nw_out, act, act_sem, sem):
    copies = [
        pltpu.make_async_copy(src, dst, sem.at[i])
        for i, (src, dst) in enumerate(((ma, nm_out), (mo, nmo_out), (se, ns_out), (nw, nw_out)))
    ]
    for copy in copies:
        copy.start()
    last = lax.axis_index("seq") * 4 + lax.axis_index("mp") == 63
    rows = lax.broadcasted_iota(jnp.int32, (512, 512), 0)
    cols = lax.broadcasted_iota(jnp.int32, (512, 512), 1)
    put = jnp.where(rows == 4 * (cols % 128) + cols // 128 - 3, 1.0, 0.0).astype(BF16)
    line = lax.broadcasted_iota(jnp.int32, (16, 512), 0)
    for t in range(4):
        span = pl.ds(t * 512, 512)
        out = jnp.dot(put, r_ref[:, span], preferred_element_type=F32)
        act[0:496, span] = out[0:496].astype(BF16)
        tail = out[496:512]
        for p in range(3):
            row = jnp.where(last, 0.0, b_ref[p:p + 1, span])
            tail = jnp.where(line == 13 + p, row, tail)
        act[496:512, span] = tail.astype(BF16)
        copy = pltpu.make_async_copy(act.at[:, span], act_out.at[:, span], act_sem.at[t])
        copy.start()
        copies.append(copy)
    for copy in copies:
        copy.wait()


def per_device(shortening_input, coarse_grad, weight_copy, master, moment, second):
    x = shortening_input[0]
    g = coarse_grad[0]
    fine, features = x.shape
    width = g.shape[1]
    w = weight_copy.reshape(2, features, width)
    rows = master.shape[1]
    scale = 1.0 / math.sqrt(lax.axis_size("dp") * lax.axis_size("seq") * g.shape[0])
    any_spec = pl.BlockSpec(memory_space=pl.ANY)
    vm = pltpu.VMEM
    held = pl.pallas_call(
        functools.partial(kernel, scale),
        out_shape=(
            vm((fine, features), BF16),
            vm((4, features), F32),
            vm((rows, width), F32),
            vm((rows, width), F32),
            vm((rows, width), F32),
            vm((2, rows, width), BF16),
        ),
        in_specs=[any_spec] * 6,
        out_specs=[pl.BlockSpec(memory_space=pltpu.VMEM)] * 6,
        scratch_shapes=[
            vm((512, 2048), BF16),
            vm((8, 4, 4, 64, 128), BF16),
            vm((8, 4, 4, 64, 128), BF16),
            vm((2, 4, 4, 64, 128), BF16),
            vm((8, 512, 1024), BF16),
            vm((2048, 1024), BF16),
            vm((2048, 1024), BF16),
            vm((2, 4, 128, 2048), BF16),
            vm((8, 128, 2048), BF16),
            vm((2, 128, 2048), BF16),
            vm((4, 2, 4, 4, 64, 512), BF16),
            vm((4, 2, 2, 2, 64, 512), BF16),
            vm((4, 2, 2, 4, 64, 512), BF16),
            vm((4, 2, 4, 64, 512), BF16),
            vm((4, 2, 2, 32, 512), BF16),
            vm((4, 2, 2, 64, 512), BF16),
            vm((4, 2, 64, 512), BF16),
            vm((4, 2, 64, 512), BF16),
            vm((4, 2048), F32),
            pltpu.SemaphoreType.DMA((COPIES,)),
            pltpu.SemaphoreType.DMA((COPIES,)),
            pltpu.SemaphoreType.DMA((LOCALS,)),
        ],
        compiler_params=pltpu.CompilerParams(
            collective_id=0, has_side_effects=True, vmem_limit_bytes=57_500_000
        ),
    )(x, g, w, master[0], moment[0], second[0])
    act, new_master, new_moment, new_second, new_weight = pl.pallas_call(
        finish,
        out_shape=(
            jax.ShapeDtypeStruct((fine, features), BF16),
            jax.ShapeDtypeStruct((rows, width), F32),
            jax.ShapeDtypeStruct((rows, width), F32),
            jax.ShapeDtypeStruct((rows, width), F32),
            jax.ShapeDtypeStruct((2, rows, width), BF16),
        ),
        in_specs=[pl.BlockSpec(memory_space=pltpu.VMEM)] * 2 + [any_spec] * 4,
        out_specs=[any_spec] * 5,
        scratch_shapes=[
            vm((fine, features), BF16),
            pltpu.SemaphoreType.DMA((4,)),
            pltpu.SemaphoreType.DMA((4,)),
        ],
        compiler_params=pltpu.CompilerParams(vmem_limit_bytes=16_000_000),
    )(*held)
    return (act[None], new_master[None], new_moment[None], new_second[None], new_weight)


def solution(mesh):
    return jax.shard_map(
        per_device,
        mesh=mesh,
        in_specs=(
            P("dp", ("seq", "mp"), None),
            P("dp", "seq", "mp"),
            P("dp", None, "mp"),
            P("dp", "seq", "mp"),
            P("dp", "seq", "mp"),
            P("dp", "seq", "mp"),
        ),
        out_specs=(
            P("dp", ("seq", "mp"), None),
            P("dp", "seq", "mp"),
            P("dp", "seq", "mp"),
            P("dp", "seq", "mp"),
            P(None, "seq", "mp"),
        ),
        check_vma=False,
    )
```

```python
import functools
import math

import jax
import jax.numpy as jnp
from jax import lax
from jax.experimental import pallas as pl
from jax.experimental.pallas import tpu as pltpu
from jax.sharding import PartitionSpec as P

MESH = pl.DeviceIdType.MESH
SHORT = 4
SIDE = 4

first_beta = 0.9
second_beta = 0.95
first_fix = 1.0 - 0.9**10
second_fix = 1.0 - 0.95**10
adam_eps = 1e-08
learn_rate = 0.05
weight_decay = 0.1

COPIES = 160
OWNED = 152
LOCALS = 16

F32 = jnp.float32
BF16 = jnp.bfloat16


def kernel(
    scale, x_hbm, g_hbm, w_hbm, ma_hbm, mo_hbm, se_hbm,
    rbuf, brecv, ma, mo, se, nw,
    xf, xall, x2t, xrel, gall, wown, wsib, pbuf, actr, arel,
    dwp, r1, r2, st, r3, r4, rsend, gr, bsend,
    send_sem, recv_sem, local_sem,
):
    d = lax.axis_index("dp")
    s = lax.axis_index("seq")
    m = lax.axis_index("mp")
    z, y = s // SIDE, s % SIDE
    h, c = m // 2, m % 2
    od, oh, oc = 1 - d, 1 - h, 1 - c

    def near(dd, hh, cc):
        return {"dp": dd, "mp": 2 * hh + cc}

    def slot(dd, hh, cc):
        return 4 * dd + 2 * hh + cc

    me = slot(d, h, c)
    sibling = near(d, h, oc)
    intra, intra_o = near(od, h, c), near(od, h, oc)
    inter, inter_o = near(od, oh, c), near(od, oh, oc)

    def at_seq(zz, yy):
        return {"seq": zz * SIDE + yy}

    up = lambda v: (v + 1) % SIDE
    down = lambda v: (v + SIDE - 1) % SIDE
    across = lambda v: (v + 2) % SIDE
    zp, zm = at_seq(up(z), y), at_seq(down(z), y)
    yp, ym = at_seq(z, up(y)), at_seq(z, down(y))
    total = 64
    place = s * 4 + m
    before = (place + total - 1) % total
    after = (place + 1) % total
    prev_dev = {"seq": before // 4, "mp": before % 4}
    next_dev = {"seq": after // 4, "mp": after % 4}

    sent, maybe, ids, local_ids = [], [], {}, {}

    def send(name, src, dst, device):
        i = ids.setdefault(name, len(ids))
        copy = pltpu.make_async_remote_copy(
            src_ref=src, dst_ref=dst, send_sem=send_sem.at[i], recv_sem=recv_sem.at[i],
            device_id=device, device_id_type=MESH,
        )
        copy.start()
        sent.append(copy)

    def arrived(name, dst):
        i = ids.setdefault(name, len(ids))
        pltpu.make_async_remote_copy(
            src_ref=dst, dst_ref=dst, send_sem=send_sem.at[i], recv_sem=recv_sem.at[i],
            device_id=sibling, device_id_type=MESH,
        ).wait_recv()

    def local(name, src, dst):
        copy = pltpu.make_async_copy(src, dst, local_sem.at[local_ids.setdefault(name, len(local_ids))])
        copy.start()
        return copy

    in_x = local("x", x_hbm, xf)
    in_g = local("g", g_hbm, gall.at[me])
    in_w = local("w", w_hbm.at[c], wown)
    in_ma = local("ma", ma_hbm, ma)
    in_mo = local("mo", mo_hbm, mo)
    in_se = local("se", se_hbm, se)

    barrier = pltpu.get_barrier_semaphore()
    partners = (sibling, intra, intra_o, inter, inter_o, zp, zm, yp, ym, prev_dev, next_dev)
    for device in partners:
        pl.semaphore_signal(barrier, inc=1, device_id=device, device_id_type=MESH)
    alone = z == m

    def owner_device(j):
        return {"seq": m * SIDE + y, "mp": j}

    def source_device(j):
        return {"seq": j * SIDE + y, "mp": z}

    for j in range(SIDE):
        for device in (owner_device(j), source_device(j)):
            pl.semaphore_signal(barrier, inc=1, device_id=device, device_id_type=MESH)
    pl.semaphore_wait(barrier, len(partners) + 2 * SIDE)

    span = (pl.ds(0, 512), pl.ds(512, 512))

    def send_g(name, half, device):
        send(name, g_hbm.at[:, span[half]], gall.at[me, :, span[half]], device)

    send_g("Gi0", 0, intra)
    send_g("Gx1", 1, inter)
    send("Gs", g_hbm, gall.at[me], sibling)
    send("W", w_hbm.at[oc], wsib, sibling)

    in_x.wait()

    def turn(i, carry):
        p, tile = i // 4, i % 4
        rows = lax.broadcasted_iota(jnp.int32, (128, 512), 0)
        cols = lax.broadcasted_iota(jnp.int32, (128, 512), 1)
        pick = jnp.where(cols == 4 * rows + p, 1.0, 0.0).astype(BF16)
        got = jnp.dot(pick, xf[:, pl.ds(pl.multiple_of(tile * 512, 512), 512)], preferred_element_type=F32)
        turned = got.T.astype(BF16)
        for j in range(4):
            block = turned[j * 128:(j + 1) * 128].reshape(2, 64, 128)
            xall[p * 2 + tile // 2, (tile % 2) * 2 + j // 2, pl.ds((j % 2) * 2, 2)] = block
        return carry

    lax.fori_loop(0, 16, turn, 0)
    own_x = local("xown", xall.at[me], x2t.at[me])
    send("Xb", xall.at[slot(d, oh, oc)], xrel.at[1], inter)
    send("Xa", xall.at[slot(d, oh, c)], xrel.at[0], intra)
    send("Xi0", xall.at[slot(od, h, c)], x2t.at[me], intra)
    send("Xi1", xall.at[slot(od, h, oc)], x2t.at[me], intra_o)
    send("Xx0", xall.at[slot(od, oh, c)], x2t.at[me], inter)
    send("Xx1", xall.at[slot(od, oh, oc)], x2t.at[me], inter_o)
    send("Xs", xall.at[slot(d, h, oc)], x2t.at[me], sibling)

    def act_part(dd, start, stop):
        def step(t, carry):
            outs = pl.ds(pl.multiple_of(t * 256, 256), 256)
            dims = (((1,), (1,)), ((), ()))
            part = lax.dot_general(gall[4 * dd + m], wown[outs, :], dims, preferred_element_type=F32)
            part += lax.dot_general(gall[4 * dd + 2 * h + oc], wsib[outs, :], dims, preferred_element_type=F32)
            pbuf[dd, :, :, outs] = part.astype(BF16).reshape(4, 128, 256)
            return carry

        lax.fori_loop(start, stop, step, 0)

    def grad_tile(ch, group_a, group_b):
        side = h if ch < 2 else oh

        def step(t, carry):
            cols = pl.ds(pl.multiple_of(t * 256, 256), 256)
            wide_cols = pl.ds(pl.multiple_of(ch % 2 * 512 + t * 256, 256), 256)

            def product(rows, column):
                left = jnp.concatenate([rows(k).reshape(256, 128) for k in range(8)], axis=1)
                right = jnp.concatenate(
                    [gall[2 * side + column, :, wide_cols], gall[4 + 2 * side + column, :, wide_cols]], axis=0
                )
                part = jnp.dot(left, right, preferred_element_type=F32)
                return part.astype(BF16).reshape(4, 64, 256)

            dwp[ch, 0, group_a, :, :, cols] = product(lambda k: x2t[k, :, group_a], 0)
            dwp[ch, 1, group_b, :, :, cols] = product(lambda k: x2t[k, group_b], 1)
            return carry

        lax.fori_loop(0, 2, step, 0)

    def wide(v):
        return v.astype(F32)

    halves = (("A", z, y, zp, zm, yp, ym), ("B", y, z, yp, ym, zp, zm))

    def reduce_1(ch):
        for i, (tag, a1, a2, p1, m1, p2, m2) in enumerate(halves):
            tag += str(ch)
            send(tag + "1p", dwp.at[ch, i, across(a1), pl.ds(0, 2)], r1.at[ch, i, 0], p1)
            send(tag + "1m", dwp.at[ch, i, across(a1), pl.ds(2, 2)], r1.at[ch, i, 1], m1)

    def reduce_2(ch):
        for i, (tag, a1, a2, p1, m1, p2, m2) in enumerate(halves):
            tag += str(ch)
            arrived(tag + "1p", r1.at[ch, i, 0])
            for j in range(2):
                dwp[ch, i, up(a1), j] = (wide(dwp[ch, i, up(a1), j]) + wide(r1[ch, i, 0, j])).astype(BF16)
            send(tag + "2p", dwp.at[ch, i, up(a1)], r2.at[ch, i, 0], p1)
            arrived(tag + "1m", r1.at[ch, i, 1])
            for j in range(2):
                dwp[ch, i, down(a1), 2 + j] = (
                    wide(dwp[ch, i, down(a1), 2 + j]) + wide(r1[ch, i, 1, j])
                ).astype(BF16)
            send(tag + "2m", dwp.at[ch, i, down(a1)], r2.at[ch, i, 1], m1)

    def reduce_3(ch):
        for i, (tag, a1, a2, p1, m1, p2, m2) in enumerate(halves):
            tag += str(ch)
            arrived(tag + "2p", r2.at[ch, i, 0])
            arrived(tag + "2m", r2.at[ch, i, 1])
            for j in range(4):
                st[ch, i, j] = (
                    wide(dwp[ch, i, a1, j]) + wide(r2[ch, i, 0, j]) + wide(r2[ch, i, 1, j])
                ).astype(BF16)
            send(tag + "3p", st.at[ch, i, across(a2), pl.ds(0, 32)], r3.at[ch, i, 0], p2)
            send(tag + "3m", st.at[ch, i, across(a2), pl.ds(32, 32)], r3.at[ch, i, 1], m2)

    def reduce_4(ch):
        for i, (tag, a1, a2, p1, m1, p2, m2) in enumerate(halves):
            tag += str(ch)
            arrived(tag + "3p", r3.at[ch, i, 0])
            st[ch, i, up(a2), 0:32] = (wide(st[ch, i, up(a2), 0:32]) + wide(r3[ch, i, 0])).astype(BF16)
            send(tag + "4p", st.at[ch, i, up(a2)], r4.at[ch, i, 0], p2)
            arrived(tag + "3m", r3.at[ch, i, 1])
            st[ch, i, down(a2), 32:64] = (
                wide(st[ch, i, down(a2), 32:64]) + wide(r3[ch, i, 1])
            ).astype(BF16)
            send(tag + "4m", st.at[ch, i, down(a2)], r4.at[ch, i, 1], m2)

    def hand_over(ch):
        for i, (tag, a1, a2, p1, m1, p2, m2) in enumerate(halves):
            tag += str(ch)
            arrived(tag + "4p", r4.at[ch, i, 0])
            arrived(tag + "4m", r4.at[ch, i, 1])
            rsend[ch, i] = (wide(st[ch, i, a2]) + wide(r4[ch, i, 0]) + wide(r4[ch, i, 1])).astype(BF16)
            column = 2 * (h if ch < 2 else oh) + i
            mark = OWNED + 2 * z + ch % 2
            home = gr.at[z, ch % 2]
            k = ids.setdefault("R" + tag, len(ids))
            copy = pltpu.make_async_remote_copy(
                src_ref=rsend.at[ch, i], dst_ref=home, send_sem=send_sem.at[k], recv_sem=recv_sem.at[mark],
                device_id=owner_device(column), device_id_type=MESH,
            )
            if ch >= 2:
                copy.start()
                sent.append(copy)
                continue
            mine = alone & (c == i)
            maybe.append((mine, copy))

            @pl.when(jnp.logical_not(mine))
            def _():
                copy.start()

            @pl.when(mine)
            def _():
                pltpu.make_async_copy(rsend.at[ch, i], home, recv_sem.at[mark]).start()

    def update(half):
        cols = slice(512 * half, 512 * half + 512)
        for j in range(SIDE):
            rows = slice(64 * j, 64 * j + 64)
            mark = OWNED + 2 * j + half
            pltpu.make_async_remote_copy(
                src_ref=gr.at[j, half], dst_ref=gr.at[j, half], send_sem=send_sem.at[mark],
                recv_sem=recv_sem.at[mark], device_id=sibling, device_id_type=MESH,
            ).wait_recv()
            grad = wide(gr[j, half]) * scale
            new_moment = first_beta * mo[rows, cols] + (1.0 - first_beta) * grad
            new_second = second_beta * se[rows, cols] + (1.0 - second_beta) * grad * grad
            ratio = new_moment / first_fix / (jnp.sqrt(new_second / second_fix) + adam_eps)
            old = ma[rows, cols]
            new_master = old - learn_rate * (ratio + weight_decay * old)
            mo[rows, cols] = new_moment
            se[rows, cols] = new_second
            ma[rows, cols] = new_master
            nw[d, rows, cols] = new_master.astype(BF16)
        send("nw" + str(half), nw.at[d, :, span[half]], nw.at[d, :, span[half]], intra)

    def pass_on(name, came, dst):
        arrived(came, dst)
        send(name, dst, dst, sibling)

    def piece(k, half):
        return gall.at[k, :, span[half]]

    def tiles(ch):
        grad_tile(ch, across(z), across(y))
        reduce_1(ch)
        grad_tile(ch, up(z), up(y))
        grad_tile(ch, down(z), down(y))
        grad_tile(ch, z, y)

    in_g.wait()
    in_w.wait()
    arrived("Gs", gall.at[slot(d, h, oc)])
    arrived("W", wsib)
    act_part(d, 0, 8)
    arrived("Xb", xrel.at[1])
    send("Xb2", xrel.at[1], x2t.at[slot(od, oh, c)], intra_o)
    send_g("Gi1", 1, intra)
    pass_on("Fi0", "Gi0", piece(slot(od, h, c), 0))
    pass_on("Fx1", "Gx1", piece(slot(od, oh, c), 1))
    send("Gb", piece(slot(od, oh, c), 1), piece(slot(od, oh, c), 1), intra)
    arrived("Xa", xrel.at[0])
    send("Xa2", xrel.at[0], x2t.at[slot(od, h, c)], inter)
    send_g("Gx0", 0, inter)
    send("Ga", piece(slot(od, h, c), 0), piece(slot(od, h, c), 0), inter)

    own_x.wait()
    arrived("Xs", x2t.at[slot(d, h, oc)])
    arrived("Xi0", x2t.at[slot(od, h, c)])
    arrived("Xi1", x2t.at[slot(od, h, oc)])
    arrived("Xx0", x2t.at[slot(od, oh, c)])
    arrived("Xx1", x2t.at[slot(od, oh, oc)])
    arrived("Xa2", x2t.at[slot(d, oh, c)])
    arrived("Xb2", x2t.at[slot(d, oh, oc)])
    arrived("Fi0", piece(slot(od, h, oc), 0))
    tiles(0)
    reduce_2(0)
    send("Pd1", pbuf.at[d, 2 * oh + oc], arel.at[1], inter)
    send("Pd0", pbuf.at[d, 2 * oh + c], arel.at[0], intra)
    send("Pa", pbuf.at[d, 2 * h + oc], actr.at[me], sibling)

    pass_on("Fi1", "Gi1", piece(slot(od, h, c), 1))
    arrived("Fi1", piece(slot(od, h, oc), 1))
    tiles(1)
    reduce_3(0)
    act_part(od, 0, 2)
    reduce_2(1)
    pass_on("Fx0", "Gx0", piece(slot(od, oh, c), 0))
    act_part(od, 2, 4)
    reduce_4(0)
    act_part(od, 4, 6)
    pass_on("Fb", "Gb", piece(slot(d, oh, c), 1))
    act_part(od, 6, 8)
    send("Pb0", pbuf.at[od, 2 * h + c], actr.at[me], intra)
    send("Pb1", pbuf.at[od, 2 * h + oc], actr.at[me], intra_o)
    send("Pc0", pbuf.at[od, 2 * oh + c], actr.at[me], inter)
    send("Pc1", pbuf.at[od, 2 * oh + oc], actr.at[me], inter_o)
    pass_on("Fa", "Ga", piece(slot(d, oh, c), 0))
    arrived("Fx1", piece(slot(od, oh, oc), 1))
    arrived("Fb", piece(slot(d, oh, oc), 1))
    tiles(3)
    arrived("Fx0", piece(slot(od, oh, oc), 0))
    arrived("Fa", piece(slot(d, oh, oc), 0))
    grad_tile(2, across(z), across(y))
    reduce_1(2)
    reduce_3(1)
    reduce_2(3)
    hand_over(0)
    grad_tile(2, up(z), up(y))
    grad_tile(2, down(z), down(y))
    grad_tile(2, z, y)
    reduce_2(2)
    reduce_4(1)
    reduce_3(3)
    hand_over(1)
    reduce_4(3)
    in_ma.wait()
    in_mo.wait()
    in_se.wait()
    hand_over(3)
    reduce_3(2)
    reduce_4(2)
    hand_over(2)
    arrived("Pd1", arel.at[1])
    send("Pf1", arel.at[1], actr.at[slot(od, oh, c)], intra_o)
    arrived("Pd0", arel.at[0])
    send("Pf0", arel.at[0], actr.at[slot(od, h, c)], inter)
    update(1)
    update(0)

    arrived("Pa", actr.at[slot(d, h, oc)])
    arrived("Pb0", actr.at[slot(od, h, c)])
    arrived("Pb1", actr.at[slot(od, h, oc)])
    arrived("Pc0", actr.at[slot(od, oh, c)])
    arrived("Pc1", actr.at[slot(od, oh, oc)])
    arrived("Pf0", actr.at[slot(d, oh, c)])
    arrived("Pf1", actr.at[slot(d, oh, oc)])
    actr[me] = pbuf[d, m]
    for p in range(4):
        k = 4 * (p // 2) + p % 2
        both = wide(actr[k]) + wide(actr[k + 2])
        rbuf[p * 128:(p + 1) * 128, :] = both.astype(BF16)
        bsend[p:p + 1, :] = both[0:1]
    send("bnd", bsend, brecv, prev_dev)
    arrived("bnd", brecv)
    for j in range(2):
        arrived("nw" + str(j), nw.at[od, :, span[j]])
    for mine, copy in maybe:

        @pl.when(jnp.logical_not(mine))
        def _():
            copy.wait_send()

    for copy in sent:
        copy.wait_send()


def finish(r_ref, b_ref, ma, mo, se, nw, act_out, nm_out, nmo_out, ns_out, nw_out, act, act_sem, sem):
    copies = [
        pltpu.make_async_copy(src, dst, sem.at[i])
        for i, (src, dst) in enumerate(((ma, nm_out), (mo, nmo_out), (se, ns_out), (nw, nw_out)))
    ]
    for copy in copies:
        copy.start()
    last = lax.axis_index("seq") * 4 + lax.axis_index("mp") == 63
    rows = lax.broadcasted_iota(jnp.int32, (512, 512), 0)
    cols = lax.broadcasted_iota(jnp.int32, (512, 512), 1)
    put = jnp.where(rows == 4 * (cols % 128) + cols // 128 - 3, 1.0, 0.0).astype(BF16)
    line = lax.broadcasted_iota(jnp.int32, (16, 512), 0)
    for t in range(4):
        span = pl.ds(t * 512, 512)
        out = jnp.dot(put, r_ref[:, span], preferred_element_type=F32)
        act[0:496, span] = out[0:496].astype(BF16)
        tail = out[496:512]
        for p in range(3):
            row = jnp.where(last, 0.0, b_ref[p:p + 1, span])
            tail = jnp.where(line == 13 + p, row, tail)
        act[496:512, span] = tail.astype(BF16)
        copy = pltpu.make_async_copy(act.at[:, span], act_out.at[:, span], act_sem.at[t])
        copy.start()
        copies.append(copy)
    for copy in copies:
        copy.wait()


def per_device(shortening_input, coarse_grad, weight_copy, master, moment, second):
    x = shortening_input[0]
    g = coarse_grad[0]
    fine, features = x.shape
    width = g.shape[1]
    w = weight_copy.reshape(2, features, width)
    rows = master.shape[1]
    scale = 1.0 / math.sqrt(lax.axis_size("dp") * lax.axis_size("seq") * g.shape[0])
    any_spec = pl.BlockSpec(memory_space=pl.ANY)
    vm = pltpu.VMEM
    held = pl.pallas_call(
        functools.partial(kernel, scale),
        out_shape=(
            vm((fine, features), BF16),
            vm((4, features), F32),
            vm((rows, width), F32),
            vm((rows, width), F32),
            vm((rows, width), F32),
            vm((2, rows, width), BF16),
        ),
        in_specs=[any_spec] * 6,
        out_specs=[pl.BlockSpec(memory_space=pltpu.VMEM)] * 6,
        scratch_shapes=[
            vm((512, 2048), BF16),
            vm((8, 4, 4, 64, 128), BF16),
            vm((8, 4, 4, 64, 128), BF16),
            vm((2, 4, 4, 64, 128), BF16),
            vm((8, 512, 1024), BF16),
            vm((2048, 1024), BF16),
            vm((2048, 1024), BF16),
            vm((2, 4, 128, 2048), BF16),
            vm((8, 128, 2048), BF16),
            vm((2, 128, 2048), BF16),
            vm((4, 2, 4, 4, 64, 512), BF16),
            vm((4, 2, 2, 2, 64, 512), BF16),
            vm((4, 2, 2, 4, 64, 512), BF16),
            vm((4, 2, 4, 64, 512), BF16),
            vm((4, 2, 2, 32, 512), BF16),
            vm((4, 2, 2, 64, 512), BF16),
            vm((4, 2, 64, 512), BF16),
            vm((4, 2, 64, 512), BF16),
            vm((4, 2048), F32),
            pltpu.SemaphoreType.DMA((COPIES,)),
            pltpu.SemaphoreType.DMA((COPIES,)),
            pltpu.SemaphoreType.DMA((LOCALS,)),
        ],
        compiler_params=pltpu.CompilerParams(
            collective_id=0, has_side_effects=True, vmem_limit_bytes=57_500_000
        ),
    )(x, g, w, master[0], moment[0], second[0])
    act, new_master, new_moment, new_second, new_weight = pl.pallas_call(
        finish,
        out_shape=(
            jax.ShapeDtypeStruct((fine, features), BF16),
            jax.ShapeDtypeStruct((rows, width), F32),
            jax.ShapeDtypeStruct((rows, width), F32),
            jax.ShapeDtypeStruct((rows, width), F32),
            jax.ShapeDtypeStruct((2, rows, width), BF16),
        ),
        in_specs=[pl.BlockSpec(memory_space=pltpu.VMEM)] * 2 + [any_spec] * 4,
        out_specs=[any_spec] * 5,
        scratch_shapes=[
            vm((fine, features), BF16),
            pltpu.SemaphoreType.DMA((4,)),
            pltpu.SemaphoreType.DMA((4,)),
        ],
        compiler_params=pltpu.CompilerParams(vmem_limit_bytes=16_000_000),
    )(*held)
    return (act[None], new_master[None], new_moment[None], new_second[None], new_weight)


def solution(mesh):
    return jax.shard_map(
        per_device,
        mesh=mesh,
        in_specs=(
            P("dp", ("seq", "mp"), None),
            P("dp", "seq", "mp"),
            P("dp", None, "mp"),
            P("dp", "seq", "mp"),
            P("dp", "seq", "mp"),
            P("dp", "seq", "mp"),
        ),
        out_specs=(
            P("dp", ("seq", "mp"), None),
            P("dp", "seq", "mp"),
            P("dp", "seq", "mp"),
            P("dp", "seq", "mp"),
            P(None, "seq", "mp"),
        ),
        check_vma=False,
    )
```

```python
import functools
import math

import jax
import jax.numpy as jnp
from jax import lax
from jax.experimental import pallas as pl
from jax.experimental.pallas import tpu as pltpu
from jax.sharding import PartitionSpec as P

MESH = pl.DeviceIdType.MESH
SHORT = 4
SIDE = 4

first_beta = 0.9
second_beta = 0.95
first_fix = 1.0 - 0.9**10
second_fix = 1.0 - 0.95**10
adam_eps = 1e-08
learn_rate = 0.05
weight_decay = 0.1

COPIES = 160
OWNED = 152
LOCALS = 16

F32 = jnp.float32
BF16 = jnp.bfloat16


def kernel(
    scale, x_hbm, g_hbm, w_hbm, ma_hbm, mo_hbm, se_hbm,
    rbuf, brecv, ma, mo, se, nw,
    xf, xall, x2t, xrel, gall, wown, wsib, pbuf, actr, arel,
    dwp, r1, r2, st, r3, r4, rsend, gr, bsend,
    send_sem, recv_sem, local_sem,
):
    d = lax.axis_index("dp")
    s = lax.axis_index("seq")
    m = lax.axis_index("mp")
    z, y = s // SIDE, s % SIDE
    h, c = m // 2, m % 2
    od, oh, oc = 1 - d, 1 - h, 1 - c

    def near(dd, hh, cc):
        return {"dp": dd, "mp": 2 * hh + cc}

    def slot(dd, hh, cc):
        return 4 * dd + 2 * hh + cc

    me = slot(d, h, c)
    sibling = near(d, h, oc)
    intra, intra_o = near(od, h, c), near(od, h, oc)
    inter, inter_o = near(od, oh, c), near(od, oh, oc)

    def at_seq(zz, yy):
        return {"seq": zz * SIDE + yy}

    up = lambda v: (v + 1) % SIDE
    down = lambda v: (v + SIDE - 1) % SIDE
    across = lambda v: (v + 2) % SIDE
    zp, zm = at_seq(up(z), y), at_seq(down(z), y)
    yp, ym = at_seq(z, up(y)), at_seq(z, down(y))
    total = 64
    place = s * 4 + m
    before = (place + total - 1) % total
    after = (place + 1) % total
    prev_dev = {"seq": before // 4, "mp": before % 4}
    next_dev = {"seq": after // 4, "mp": after % 4}

    sent, maybe, ids, local_ids = [], [], {}, {}

    def send(name, src, dst, device):
        i = ids.setdefault(name, len(ids))
        copy = pltpu.make_async_remote_copy(
            src_ref=src, dst_ref=dst, send_sem=send_sem.at[i], recv_sem=recv_sem.at[i],
            device_id=device, device_id_type=MESH,
        )
        copy.start()
        sent.append(copy)

    def arrived(name, dst):
        i = ids.setdefault(name, len(ids))
        pltpu.make_async_remote_copy(
            src_ref=dst, dst_ref=dst, send_sem=send_sem.at[i], recv_sem=recv_sem.at[i],
            device_id=sibling, device_id_type=MESH,
        ).wait_recv()

    def local(name, src, dst):
        copy = pltpu.make_async_copy(src, dst, local_sem.at[local_ids.setdefault(name, len(local_ids))])
        copy.start()
        return copy

    in_x = local("x", x_hbm, xf)
    in_g = local("g", g_hbm, gall.at[me])
    in_w = local("w", w_hbm.at[c], wown)
    in_ma = local("ma", ma_hbm, ma)
    in_mo = local("mo", mo_hbm, mo)
    in_se = local("se", se_hbm, se)

    barrier = pltpu.get_barrier_semaphore()
    partners = (sibling, intra, intra_o, inter, inter_o, zp, zm, yp, ym, prev_dev, next_dev)
    for device in partners:
        pl.semaphore_signal(barrier, inc=1, device_id=device, device_id_type=MESH)
    alone = z == m

    def owner_device(j):
        return {"seq": m * SIDE + y, "mp": j}

    def source_device(j):
        return {"seq": j * SIDE + y, "mp": z}

    for j in range(SIDE):
        for device in (owner_device(j), source_device(j)):
            pl.semaphore_signal(barrier, inc=1, device_id=device, device_id_type=MESH)
    pl.semaphore_wait(barrier, len(partners) + 2 * SIDE)

    span = (pl.ds(0, 512), pl.ds(512, 512))

    def send_g(name, half, device):
        send(name, g_hbm.at[:, span[half]], gall.at[me, :, span[half]], device)

    send_g("Gi0", 0, intra)
    send("Gs", g_hbm, gall.at[me], sibling)
    send("W", w_hbm.at[oc], wsib, sibling)

    in_x.wait()

    def turn(i, carry):
        p, tile = i // 4, i % 4
        rows = lax.broadcasted_iota(jnp.int32, (128, 512), 0)
        cols = lax.broadcasted_iota(jnp.int32, (128, 512), 1)
        pick = jnp.where(cols == 4 * rows + p, 1.0, 0.0).astype(BF16)
        got = jnp.dot(pick, xf[:, pl.ds(pl.multiple_of(tile * 512, 512), 512)], preferred_element_type=F32)
        turned = got.T.astype(BF16)
        for j in range(4):
            block = turned[j * 128:(j + 1) * 128].reshape(2, 64, 128)
            xall[p * 2 + tile // 2, (tile % 2) * 2 + j // 2, pl.ds((j % 2) * 2, 2)] = block
        return carry

    lax.fori_loop(0, 16, turn, 0)
    own_x = local("xown", xall.at[me], x2t.at[me])
    send("Xb", xall.at[slot(d, oh, oc)], xrel.at[1], inter)
    send("Xa", xall.at[slot(d, oh, c)], xrel.at[0], intra)
    send("Xi0", xall.at[slot(od, h, c)], x2t.at[me], intra)
    send("Xi1", xall.at[slot(od, h, oc)], x2t.at[me], intra_o)
    send("Xx0", xall.at[slot(od, oh, c)], x2t.at[me], inter)
    send("Xx1", xall.at[slot(od, oh, oc)], x2t.at[me], inter_o)
    send("Xs", xall.at[slot(d, h, oc)], x2t.at[me], sibling)

    def act_part(dd, start, stop):
        def step(t, carry):
            outs = pl.ds(pl.multiple_of(t * 256, 256), 256)
            dims = (((1,), (1,)), ((), ()))
            part = lax.dot_general(gall[4 * dd + m], wown[outs, :], dims, preferred_element_type=F32)
            part += lax.dot_general(gall[4 * dd + 2 * h + oc], wsib[outs, :], dims, preferred_element_type=F32)
            pbuf[dd, :, :, outs] = part.astype(BF16).reshape(4, 128, 256)
            return carry

        lax.fori_loop(start, stop, step, 0)

    def grad_tile(ch, group_a, group_b):
        side = h if ch < 2 else oh

        def step(t, carry):
            cols = pl.ds(pl.multiple_of(t * 256, 256), 256)
            wide_cols = pl.ds(pl.multiple_of(ch % 2 * 512 + t * 256, 256), 256)

            def product(rows, column):
                left = jnp.concatenate([rows(k).reshape(256, 128) for k in range(8)], axis=1)
                right = jnp.concatenate(
                    [gall[2 * side + column, :, wide_cols], gall[4 + 2 * side + column, :, wide_cols]], axis=0
                )
                part = jnp.dot(left, right, preferred_element_type=F32)
                return part.astype(BF16).reshape(4, 64, 256)

            dwp[ch, 0, group_a, :, :, cols] = product(lambda k: x2t[k, :, group_a], 0)
            dwp[ch, 1, group_b, :, :, cols] = product(lambda k: x2t[k, group_b], 1)
            return carry

        lax.fori_loop(0, 2, step, 0)

    def wide(v):
        return v.astype(F32)

    halves = (("A", z, y, zp, zm, yp, ym), ("B", y, z, yp, ym, zp, zm))

    def reduce_1(ch):
        for i, (tag, a1, a2, p1, m1, p2, m2) in enumerate(halves):
            tag += str(ch)
            send(tag + "1p", dwp.at[ch, i, across(a1), pl.ds(0, 2)], r1.at[ch, i, 0], p1)
            send(tag + "1m", dwp.at[ch, i, across(a1), pl.ds(2, 2)], r1.at[ch, i, 1], m1)

    def reduce_2(ch):
        for i, (tag, a1, a2, p1, m1, p2, m2) in enumerate(halves):
            tag += str(ch)
            arrived(tag + "1p", r1.at[ch, i, 0])
            for j in range(2):
                dwp[ch, i, up(a1), j] = (wide(dwp[ch, i, up(a1), j]) + wide(r1[ch, i, 0, j])).astype(BF16)
            send(tag + "2p", dwp.at[ch, i, up(a1)], r2.at[ch, i, 0], p1)
            arrived(tag + "1m", r1.at[ch, i, 1])
            for j in range(2):
                dwp[ch, i, down(a1), 2 + j] = (
                    wide(dwp[ch, i, down(a1), 2 + j]) + wide(r1[ch, i, 1, j])
                ).astype(BF16)
            send(tag + "2m", dwp.at[ch, i, down(a1)], r2.at[ch, i, 1], m1)

    def reduce_3(ch):
        for i, (tag, a1, a2, p1, m1, p2, m2) in enumerate(halves):
            tag += str(ch)
            arrived(tag + "2p", r2.at[ch, i, 0])
            arrived(tag + "2m", r2.at[ch, i, 1])
            for j in range(4):
                st[ch, i, j] = (
                    wide(dwp[ch, i, a1, j]) + wide(r2[ch, i, 0, j]) + wide(r2[ch, i, 1, j])
                ).astype(BF16)
            send(tag + "3p", st.at[ch, i, across(a2), pl.ds(0, 32)], r3.at[ch, i, 0], p2)
            send(tag + "3m", st.at[ch, i, across(a2), pl.ds(32, 32)], r3.at[ch, i, 1], m2)

    def reduce_4(ch):
        for i, (tag, a1, a2, p1, m1, p2, m2) in enumerate(halves):
            tag += str(ch)
            arrived(tag + "3p", r3.at[ch, i, 0])
            st[ch, i, up(a2), 0:32] = (wide(st[ch, i, up(a2), 0:32]) + wide(r3[ch, i, 0])).astype(BF16)
            send(tag + "4p", st.at[ch, i, up(a2)], r4.at[ch, i, 0], p2)
            arrived(tag + "3m", r3.at[ch, i, 1])
            st[ch, i, down(a2), 32:64] = (
                wide(st[ch, i, down(a2), 32:64]) + wide(r3[ch, i, 1])
            ).astype(BF16)
            send(tag + "4m", st.at[ch, i, down(a2)], r4.at[ch, i, 1], m2)

    def hand_over(ch):
        for i, (tag, a1, a2, p1, m1, p2, m2) in enumerate(halves):
            tag += str(ch)
            arrived(tag + "4p", r4.at[ch, i, 0])
            arrived(tag + "4m", r4.at[ch, i, 1])
            rsend[ch, i] = (wide(st[ch, i, a2]) + wide(r4[ch, i, 0]) + wide(r4[ch, i, 1])).astype(BF16)
            column = 2 * (h if ch < 2 else oh) + i
            mark = OWNED + 2 * z + ch % 2
            home = gr.at[z, ch % 2]
            k = ids.setdefault("R" + tag, len(ids))
            copy = pltpu.make_async_remote_copy(
                src_ref=rsend.at[ch, i], dst_ref=home, send_sem=send_sem.at[k], recv_sem=recv_sem.at[mark],
                device_id=owner_device(column), device_id_type=MESH,
            )
            if ch >= 2:
                copy.start()
                sent.append(copy)
                continue
            mine = alone & (c == i)
            maybe.append((mine, copy))

            @pl.when(jnp.logical_not(mine))
            def _():
                copy.start()

            @pl.when(mine)
            def _():
                pltpu.make_async_copy(rsend.at[ch, i], home, recv_sem.at[mark]).start()

    def update(half):
        cols = slice(512 * half, 512 * half + 512)
        for j in range(SIDE):
            rows = slice(64 * j, 64 * j + 64)
            mark = OWNED + 2 * j + half
            pltpu.make_async_remote_copy(
                src_ref=gr.at[j, half], dst_ref=gr.at[j, half], send_sem=send_sem.at[mark],
                recv_sem=recv_sem.at[mark], device_id=sibling, device_id_type=MESH,
            ).wait_recv()
            grad = wide(gr[j, half]) * scale
            new_moment = first_beta * mo[rows, cols] + (1.0 - first_beta) * grad
            new_second = second_beta * se[rows, cols] + (1.0 - second_beta) * grad * grad
            ratio = new_moment / first_fix / (jnp.sqrt(new_second / second_fix) + adam_eps)
            old = ma[rows, cols]
            new_master = old - learn_rate * (ratio + weight_decay * old)
            mo[rows, cols] = new_moment
            se[rows, cols] = new_second
            ma[rows, cols] = new_master
            nw[d, rows, cols] = new_master.astype(BF16)
        send("nw" + str(half), nw.at[d, :, span[half]], nw.at[d, :, span[half]], intra)

    def pass_on(name, came, dst):
        arrived(came, dst)
        send(name, dst, dst, sibling)

    def piece(k, half):
        return gall.at[k, :, span[half]]

    def tiles(ch):
        grad_tile(ch, across(z), across(y))
        reduce_1(ch)
        grad_tile(ch, up(z), up(y))
        grad_tile(ch, down(z), down(y))
        grad_tile(ch, z, y)

    arrived("Xb", xrel.at[1])
    send("Xb2", xrel.at[1], x2t.at[slot(od, oh, c)], intra_o)
    send_g("Gi1", 1, intra)
    in_g.wait()
    in_w.wait()
    arrived("Gs", gall.at[slot(d, h, oc)])
    arrived("W", wsib)
    act_part(d, 0, 8)
    arrived("Xa", xrel.at[0])
    send("Xa2", xrel.at[0], x2t.at[slot(od, h, c)], inter)
    send_g("Gx1", 1, inter)
    send_g("Gx0", 0, inter)
    pass_on("Fi0", "Gi0", piece(slot(od, h, c), 0))
    send("Ga", piece(slot(od, h, c), 0), piece(slot(od, h, c), 0), inter)

    own_x.wait()
    arrived("Xs", x2t.at[slot(d, h, oc)])
    arrived("Xi0", x2t.at[slot(od, h, c)])
    arrived("Xi1", x2t.at[slot(od, h, oc)])
    arrived("Xx0", x2t.at[slot(od, oh, c)])
    arrived("Xx1", x2t.at[slot(od, oh, oc)])
    arrived("Xa2", x2t.at[slot(d, oh, c)])
    arrived("Xb2", x2t.at[slot(d, oh, oc)])
    arrived("Fi0", piece(slot(od, h, oc), 0))
    tiles(0)
    pass_on("Fx1", "Gx1", piece(slot(od, oh, c), 1))
    send("Gb", piece(slot(od, oh, c), 1), piece(slot(od, oh, c), 1), intra)
    reduce_2(0)
    send("Pd1", pbuf.at[d, 2 * oh + oc], arel.at[1], inter)
    send("Pd0", pbuf.at[d, 2 * oh + c], arel.at[0], intra)
    send("Pa", pbuf.at[d, 2 * h + oc], actr.at[me], sibling)

    pass_on("Fi1", "Gi1", piece(slot(od, h, c), 1))
    arrived("Fi1", piece(slot(od, h, oc), 1))
    tiles(1)
    reduce_3(0)
    act_part(od, 0, 2)
    reduce_2(1)
    pass_on("Fx0", "Gx0", piece(slot(od, oh, c), 0))
    act_part(od, 2, 4)
    reduce_4(0)
    act_part(od, 4, 6)
    pass_on("Fb", "Gb", piece(slot(d, oh, c), 1))
    act_part(od, 6, 8)
    send("Pb0", pbuf.at[od, 2 * h + c], actr.at[me], intra)
    send("Pb1", pbuf.at[od, 2 * h + oc], actr.at[me], intra_o)
    send("Pc0", pbuf.at[od, 2 * oh + c], actr.at[me], inter)
    send("Pc1", pbuf.at[od, 2 * oh + oc], actr.at[me], inter_o)
    pass_on("Fa", "Ga", piece(slot(d, oh, c), 0))
    arrived("Fx1", piece(slot(od, oh, oc), 1))
    arrived("Fb", piece(slot(d, oh, oc), 1))
    tiles(3)
    arrived("Fx0", piece(slot(od, oh, oc), 0))
    arrived("Fa", piece(slot(d, oh, oc), 0))
    grad_tile(2, across(z), across(y))
    reduce_1(2)
    reduce_3(1)
    reduce_2(3)
    hand_over(0)
    grad_tile(2, up(z), up(y))
    grad_tile(2, down(z), down(y))
    grad_tile(2, z, y)
    reduce_2(2)
    reduce_4(1)
    arrived("Pd1", arel.at[1])
    send("Pf1", arel.at[1], actr.at[slot(od, oh, c)], intra_o)
    arrived("Pd0", arel.at[0])
    send("Pf0", arel.at[0], actr.at[slot(od, h, c)], inter)
    reduce_3(3)
    hand_over(1)
    reduce_4(3)
    in_ma.wait()
    in_mo.wait()
    in_se.wait()
    hand_over(3)
    reduce_3(2)
    reduce_4(2)
    hand_over(2)
    update(1)
    update(0)

    arrived("Pa", actr.at[slot(d, h, oc)])
    arrived("Pb0", actr.at[slot(od, h, c)])
    arrived("Pb1", actr.at[slot(od, h, oc)])
    arrived("Pc0", actr.at[slot(od, oh, c)])
    arrived("Pc1", actr.at[slot(od, oh, oc)])
    arrived("Pf0", actr.at[slot(d, oh, c)])
    arrived("Pf1", actr.at[slot(d, oh, oc)])
    actr[me] = pbuf[d, m]
    for p in range(4):
        k = 4 * (p // 2) + p % 2
        both = wide(actr[k]) + wide(actr[k + 2])
        rbuf[p * 128:(p + 1) * 128, :] = both.astype(BF16)
        bsend[p:p + 1, :] = both[0:1]
    send("bnd", bsend, brecv, prev_dev)
    arrived("bnd", brecv)
    for j in range(2):
        arrived("nw" + str(j), nw.at[od, :, span[j]])
    for mine, copy in maybe:

        @pl.when(jnp.logical_not(mine))
        def _():
            copy.wait_send()

    for copy in sent:
        copy.wait_send()


def finish(r_ref, b_ref, ma, mo, se, nw, act_out, nm_out, nmo_out, ns_out, nw_out, act, act_sem, sem):
    copies = [
        pltpu.make_async_copy(src, dst, sem.at[i])
        for i, (src, dst) in enumerate(((ma, nm_out), (mo, nmo_out), (se, ns_out), (nw, nw_out)))
    ]
    for copy in copies:
        copy.start()
    last = lax.axis_index("seq") * 4 + lax.axis_index("mp") == 63
    rows = lax.broadcasted_iota(jnp.int32, (512, 512), 0)
    cols = lax.broadcasted_iota(jnp.int32, (512, 512), 1)
    put = jnp.where(rows == 4 * (cols % 128) + cols // 128 - 3, 1.0, 0.0).astype(BF16)
    line = lax.broadcasted_iota(jnp.int32, (16, 512), 0)
    for t in range(4):
        span = pl.ds(t * 512, 512)
        out = jnp.dot(put, r_ref[:, span], preferred_element_type=F32)
        act[0:496, span] = out[0:496].astype(BF16)
        tail = out[496:512]
        for p in range(3):
            row = jnp.where(last, 0.0, b_ref[p:p + 1, span])
            tail = jnp.where(line == 13 + p, row, tail)
        act[496:512, span] = tail.astype(BF16)
        copy = pltpu.make_async_copy(act.at[:, span], act_out.at[:, span], act_sem.at[t])
        copy.start()
        copies.append(copy)
    for copy in copies:
        copy.wait()


def per_device(shortening_input, coarse_grad, weight_copy, master, moment, second):
    x = shortening_input[0]
    g = coarse_grad[0]
    fine, features = x.shape
    width = g.shape[1]
    w = weight_copy.reshape(2, features, width)
    rows = master.shape[1]
    scale = 1.0 / math.sqrt(lax.axis_size("dp") * lax.axis_size("seq") * g.shape[0])
    any_spec = pl.BlockSpec(memory_space=pl.ANY)
    vm = pltpu.VMEM
    held = pl.pallas_call(
        functools.partial(kernel, scale),
        out_shape=(
            vm((fine, features), BF16),
            vm((4, features), F32),
            vm((rows, width), F32),
            vm((rows, width), F32),
            vm((rows, width), F32),
            vm((2, rows, width), BF16),
        ),
        in_specs=[any_spec] * 6,
        out_specs=[pl.BlockSpec(memory_space=pltpu.VMEM)] * 6,
        scratch_shapes=[
            vm((512, 2048), BF16),
            vm((8, 4, 4, 64, 128), BF16),
            vm((8, 4, 4, 64, 128), BF16),
            vm((2, 4, 4, 64, 128), BF16),
            vm((8, 512, 1024), BF16),
            vm((2048, 1024), BF16),
            vm((2048, 1024), BF16),
            vm((2, 4, 128, 2048), BF16),
            vm((8, 128, 2048), BF16),
            vm((2, 128, 2048), BF16),
            vm((4, 2, 4, 4, 64, 512), BF16),
            vm((4, 2, 2, 2, 64, 512), BF16),
            vm((4, 2, 2, 4, 64, 512), BF16),
            vm((4, 2, 4, 64, 512), BF16),
            vm((4, 2, 2, 32, 512), BF16),
            vm((4, 2, 2, 64, 512), BF16),
            vm((4, 2, 64, 512), BF16),
            vm((4, 2, 64, 512), BF16),
            vm((4, 2048), F32),
            pltpu.SemaphoreType.DMA((COPIES,)),
            pltpu.SemaphoreType.DMA((COPIES,)),
            pltpu.SemaphoreType.DMA((LOCALS,)),
        ],
        compiler_params=pltpu.CompilerParams(
            collective_id=0, has_side_effects=True, vmem_limit_bytes=57_500_000
        ),
    )(x, g, w, master[0], moment[0], second[0])
    act, new_master, new_moment, new_second, new_weight = pl.pallas_call(
        finish,
        out_shape=(
            jax.ShapeDtypeStruct((fine, features), BF16),
            jax.ShapeDtypeStruct((rows, width), F32),
            jax.ShapeDtypeStruct((rows, width), F32),
            jax.ShapeDtypeStruct((rows, width), F32),
            jax.ShapeDtypeStruct((2, rows, width), BF16),
        ),
        in_specs=[pl.BlockSpec(memory_space=pltpu.VMEM)] * 2 + [any_spec] * 4,
        out_specs=[any_spec] * 5,
        scratch_shapes=[
            vm((fine, features), BF16),
            pltpu.SemaphoreType.DMA((4,)),
            pltpu.SemaphoreType.DMA((4,)),
        ],
        compiler_params=pltpu.CompilerParams(vmem_limit_bytes=16_000_000),
    )(*held)
    return (act[None], new_master[None], new_moment[None], new_second[None], new_weight)


def solution(mesh):
    return jax.shard_map(
        per_device,
        mesh=mesh,
        in_specs=(
            P("dp", ("seq", "mp"), None),
            P("dp", "seq", "mp"),
            P("dp", None, "mp"),
            P("dp", "seq", "mp"),
            P("dp", "seq", "mp"),
            P("dp", "seq", "mp"),
        ),
        out_specs=(
            P("dp", ("seq", "mp"), None),
            P("dp", "seq", "mp"),
            P("dp", "seq", "mp"),
            P("dp", "seq", "mp"),
            P(None, "seq", "mp"),
        ),
        check_vma=False,
    )
```

```python
import functools
import math

import jax
import jax.numpy as jnp
from jax import lax
from jax.experimental import pallas as pl
from jax.experimental.pallas import tpu as pltpu
from jax.sharding import PartitionSpec as P

MESH = pl.DeviceIdType.MESH
SHORT = 4
SIDE = 4

first_beta = 0.9
second_beta = 0.95
first_fix = 1.0 - 0.9**10
second_fix = 1.0 - 0.95**10
adam_eps = 1e-08
learn_rate = 0.05
weight_decay = 0.1

COPIES = 160
OWNED = 152
LOCALS = 16

F32 = jnp.float32
BF16 = jnp.bfloat16


def kernel(
    scale, x_hbm, g_hbm, w_hbm, ma_hbm, mo_hbm, se_hbm,
    rbuf, brecv, ma, mo, se, nw,
    xf, xall, x2t, xrel, gall, wown, wsib, pbuf, actr, arel,
    dwp, r1, r2, st, r3, r4, rsend, gr, bsend,
    send_sem, recv_sem, local_sem,
):
    d = lax.axis_index("dp")
    s = lax.axis_index("seq")
    m = lax.axis_index("mp")
    z, y = s // SIDE, s % SIDE
    h, c = m // 2, m % 2
    od, oh, oc = 1 - d, 1 - h, 1 - c

    def near(dd, hh, cc):
        return {"dp": dd, "mp": 2 * hh + cc}

    def slot(dd, hh, cc):
        return 4 * dd + 2 * hh + cc

    me = slot(d, h, c)
    sibling = near(d, h, oc)
    intra, intra_o = near(od, h, c), near(od, h, oc)
    inter, inter_o = near(od, oh, c), near(od, oh, oc)

    def at_seq(zz, yy):
        return {"seq": zz * SIDE + yy}

    up = lambda v: (v + 1) % SIDE
    down = lambda v: (v + SIDE - 1) % SIDE
    across = lambda v: (v + 2) % SIDE
    zp, zm = at_seq(up(z), y), at_seq(down(z), y)
    yp, ym = at_seq(z, up(y)), at_seq(z, down(y))
    total = 64
    place = s * 4 + m
    before = (place + total - 1) % total
    after = (place + 1) % total
    prev_dev = {"seq": before // 4, "mp": before % 4}
    next_dev = {"seq": after // 4, "mp": after % 4}

    sent, maybe, ids, local_ids = [], [], {}, {}

    def send(name, src, dst, device):
        i = ids.setdefault(name, len(ids))
        copy = pltpu.make_async_remote_copy(
            src_ref=src, dst_ref=dst, send_sem=send_sem.at[i], recv_sem=recv_sem.at[i],
            device_id=device, device_id_type=MESH,
        )
        copy.start()
        sent.append(copy)

    def arrived(name, dst):
        i = ids.setdefault(name, len(ids))
        pltpu.make_async_remote_copy(
            src_ref=dst, dst_ref=dst, send_sem=send_sem.at[i], recv_sem=recv_sem.at[i],
            device_id=sibling, device_id_type=MESH,
        ).wait_recv()

    def local(name, src, dst):
        copy = pltpu.make_async_copy(src, dst, local_sem.at[local_ids.setdefault(name, len(local_ids))])
        copy.start()
        return copy

    in_x = local("x", x_hbm, xf)
    in_g = local("g", g_hbm, gall.at[me])
    in_w = local("w", w_hbm.at[c], wown)
    in_ma = local("ma", ma_hbm, ma)
    in_mo = local("mo", mo_hbm, mo)
    in_se = local("se", se_hbm, se)

    barrier = pltpu.get_barrier_semaphore()
    partners = (sibling, intra, intra_o, inter, inter_o, zp, zm, yp, ym, prev_dev, next_dev)
    for device in partners:
        pl.semaphore_signal(barrier, inc=1, device_id=device, device_id_type=MESH)
    alone = z == m

    def owner_device(j):
        return {"seq": m * SIDE + y, "mp": j}

    def source_device(j):
        return {"seq": j * SIDE + y, "mp": z}

    for j in range(SIDE):
        for device in (owner_device(j), source_device(j)):
            pl.semaphore_signal(barrier, inc=1, device_id=device, device_id_type=MESH)
    pl.semaphore_wait(barrier, len(partners) + 2 * SIDE)

    span = (pl.ds(0, 512), pl.ds(512, 512))

    def send_g(name, half, device):
        send(name, g_hbm.at[:, span[half]], gall.at[me, :, span[half]], device)

    send_g("Gi0", 0, intra)
    send("Gs", g_hbm, gall.at[me], sibling)
    send("W", w_hbm.at[oc], wsib, sibling)

    in_x.wait()

    def turn(i, carry):
        p, tile = i // 4, i % 4
        rows = lax.broadcasted_iota(jnp.int32, (128, 512), 0)
        cols = lax.broadcasted_iota(jnp.int32, (128, 512), 1)
        pick = jnp.where(cols == 4 * rows + p, 1.0, 0.0).astype(BF16)
        got = jnp.dot(pick, xf[:, pl.ds(pl.multiple_of(tile * 512, 512), 512)], preferred_element_type=F32)
        turned = got.T.astype(BF16)
        for j in range(4):
            block = turned[j * 128:(j + 1) * 128].reshape(2, 64, 128)
            xall[p * 2 + tile // 2, (tile % 2) * 2 + j // 2, pl.ds((j % 2) * 2, 2)] = block
        return carry

    lax.fori_loop(0, 16, turn, 0)
    own_x = local("xown", xall.at[me], x2t.at[me])
    send("Xb", xall.at[slot(d, oh, oc)], xrel.at[1], inter)
    send("Xa", xall.at[slot(d, oh, c)], xrel.at[0], intra)
    send("Xi0", xall.at[slot(od, h, c)], x2t.at[me], intra)
    send("Xi1", xall.at[slot(od, h, oc)], x2t.at[me], intra_o)
    send("Xx0", xall.at[slot(od, oh, c)], x2t.at[me], inter)
    send("Xx1", xall.at[slot(od, oh, oc)], x2t.at[me], inter_o)
    send("Xs", xall.at[slot(d, h, oc)], x2t.at[me], sibling)

    def act_part(dd, start, stop):
        def step(t, carry):
            outs = pl.ds(pl.multiple_of(t * 256, 256), 256)
            dims = (((1,), (1,)), ((), ()))
            part = lax.dot_general(gall[4 * dd + m], wown[outs, :], dims, preferred_element_type=F32)
            part += lax.dot_general(gall[4 * dd + 2 * h + oc], wsib[outs, :], dims, preferred_element_type=F32)
            pbuf[dd, :, :, outs] = part.astype(BF16).reshape(4, 128, 256)
            return carry

        lax.fori_loop(start, stop, step, 0)

    def grad_tile(ch, group_a, group_b):
        side = h if ch < 2 else oh

        def step(t, carry):
            cols = pl.ds(pl.multiple_of(t * 256, 256), 256)
            wide_cols = pl.ds(pl.multiple_of(ch % 2 * 512 + t * 256, 256), 256)

            def product(rows, column):
                left = jnp.concatenate([rows(k).reshape(256, 128) for k in range(8)], axis=1)
                right = jnp.concatenate(
                    [gall[2 * side + column, :, wide_cols], gall[4 + 2 * side + column, :, wide_cols]], axis=0
                )
                part = jnp.dot(left, right, preferred_element_type=F32)
                return part.astype(BF16).reshape(4, 64, 256)

            dwp[ch, 0, group_a, :, :, cols] = product(lambda k: x2t[k, :, group_a], 0)
            dwp[ch, 1, group_b, :, :, cols] = product(lambda k: x2t[k, group_b], 1)
            return carry

        lax.fori_loop(0, 2, step, 0)

    def wide(v):
        return v.astype(F32)

    halves = (("A", z, y, zp, zm, yp, ym), ("B", y, z, yp, ym, zp, zm))

    def reduce_1(ch):
        for i, (tag, a1, a2, p1, m1, p2, m2) in enumerate(halves):
            tag += str(ch)
            send(tag + "1p", dwp.at[ch, i, across(a1), pl.ds(0, 2)], r1.at[ch, i, 0], p1)
            send(tag + "1m", dwp.at[ch, i, across(a1), pl.ds(2, 2)], r1.at[ch, i, 1], m1)

    def reduce_2(ch):
        for i, (tag, a1, a2, p1, m1, p2, m2) in enumerate(halves):
            tag += str(ch)
            arrived(tag + "1p", r1.at[ch, i, 0])
            for j in range(2):
                dwp[ch, i, up(a1), j] = (wide(dwp[ch, i, up(a1), j]) + wide(r1[ch, i, 0, j])).astype(BF16)
            send(tag + "2p", dwp.at[ch, i, up(a1)], r2.at[ch, i, 0], p1)
            arrived(tag + "1m", r1.at[ch, i, 1])
            for j in range(2):
                dwp[ch, i, down(a1), 2 + j] = (
                    wide(dwp[ch, i, down(a1), 2 + j]) + wide(r1[ch, i, 1, j])
                ).astype(BF16)
            send(tag + "2m", dwp.at[ch, i, down(a1)], r2.at[ch, i, 1], m1)

    def reduce_3(ch):
        for i, (tag, a1, a2, p1, m1, p2, m2) in enumerate(halves):
            tag += str(ch)
            arrived(tag + "2p", r2.at[ch, i, 0])
            arrived(tag + "2m", r2.at[ch, i, 1])
            for j in range(4):
                st[ch, i, j] = (
                    wide(dwp[ch, i, a1, j]) + wide(r2[ch, i, 0, j]) + wide(r2[ch, i, 1, j])
                ).astype(BF16)
            send(tag + "3p", st.at[ch, i, across(a2), pl.ds(0, 32)], r3.at[ch, i, 0], p2)
            send(tag + "3m", st.at[ch, i, across(a2), pl.ds(32, 32)], r3.at[ch, i, 1], m2)

    def reduce_4(ch):
        for i, (tag, a1, a2, p1, m1, p2, m2) in enumerate(halves):
            tag += str(ch)
            arrived(tag + "3p", r3.at[ch, i, 0])
            st[ch, i, up(a2), 0:32] = (wide(st[ch, i, up(a2), 0:32]) + wide(r3[ch, i, 0])).astype(BF16)
            send(tag + "4p", st.at[ch, i, up(a2)], r4.at[ch, i, 0], p2)
            arrived(tag + "3m", r3.at[ch, i, 1])
            st[ch, i, down(a2), 32:64] = (
                wide(st[ch, i, down(a2), 32:64]) + wide(r3[ch, i, 1])
            ).astype(BF16)
            send(tag + "4m", st.at[ch, i, down(a2)], r4.at[ch, i, 1], m2)

    def hand_over(ch):
        for i, (tag, a1, a2, p1, m1, p2, m2) in enumerate(halves):
            tag += str(ch)
            arrived(tag + "4p", r4.at[ch, i, 0])
            arrived(tag + "4m", r4.at[ch, i, 1])
            rsend[ch, i] = (wide(st[ch, i, a2]) + wide(r4[ch, i, 0]) + wide(r4[ch, i, 1])).astype(BF16)
            column = 2 * (h if ch < 2 else oh) + i
            mark = OWNED + 2 * z + ch % 2
            home = gr.at[z, ch % 2]
            k = ids.setdefault("R" + tag, len(ids))
            copy = pltpu.make_async_remote_copy(
                src_ref=rsend.at[ch, i], dst_ref=home, send_sem=send_sem.at[k], recv_sem=recv_sem.at[mark],
                device_id=owner_device(column), device_id_type=MESH,
            )
            if ch >= 2:
                copy.start()
                sent.append(copy)
                continue
            mine = alone & (c == i)
            maybe.append((mine, copy))

            @pl.when(jnp.logical_not(mine))
            def _():
                copy.start()

            @pl.when(mine)
            def _():
                pltpu.make_async_copy(rsend.at[ch, i], home, recv_sem.at[mark]).start()

    def update(half):
        cols = slice(512 * half, 512 * half + 512)
        for j in range(SIDE):
            rows = slice(64 * j, 64 * j + 64)
            mark = OWNED + 2 * j + half
            pltpu.make_async_remote_copy(
                src_ref=gr.at[j, half], dst_ref=gr.at[j, half], send_sem=send_sem.at[mark],
                recv_sem=recv_sem.at[mark], device_id=sibling, device_id_type=MESH,
            ).wait_recv()
            grad = wide(gr[j, half]) * scale
            new_moment = first_beta * mo[rows, cols] + (1.0 - first_beta) * grad
            new_second = second_beta * se[rows, cols] + (1.0 - second_beta) * grad * grad
            ratio = new_moment / first_fix / (jnp.sqrt(new_second / second_fix) + adam_eps)
            old = ma[rows, cols]
            new_master = old - learn_rate * (ratio + weight_decay * old)
            mo[rows, cols] = new_moment
            se[rows, cols] = new_second
            ma[rows, cols] = new_master
            nw[d, rows, cols] = new_master.astype(BF16)
        send("nw" + str(half), nw.at[d, :, span[half]], nw.at[d, :, span[half]], intra)

    def pass_on(name, came, dst):
        arrived(came, dst)
        send(name, dst, dst, sibling)

    def piece(k, half):
        return gall.at[k, :, span[half]]

    def quarter(k, part):
        return gall.at[k, pl.ds(256 * part, 256), span[1]]

    def tiles(ch):
        grad_tile(ch, across(z), across(y))
        reduce_1(ch)
        grad_tile(ch, up(z), up(y))
        grad_tile(ch, down(z), down(y))
        grad_tile(ch, z, y)

    arrived("Xb", xrel.at[1])
    send("Xb2", xrel.at[1], x2t.at[slot(od, oh, c)], intra_o)
    send_g("Gi1", 1, intra)
    in_g.wait()
    in_w.wait()
    arrived("Gs", gall.at[slot(d, h, oc)])
    arrived("W", wsib)
    act_part(d, 0, 8)
    arrived("Xa", xrel.at[0])
    send("Xa2", xrel.at[0], x2t.at[slot(od, h, c)], inter)
    send_g("Gx1", 1, inter)
    send_g("Gx0", 0, inter)
    pass_on("Fi0", "Gi0", piece(slot(od, h, c), 0))
    send("Ga", piece(slot(od, h, c), 0), piece(slot(od, h, c), 0), inter)

    own_x.wait()
    arrived("Xs", x2t.at[slot(d, h, oc)])
    arrived("Xi0", x2t.at[slot(od, h, c)])
    arrived("Xi1", x2t.at[slot(od, h, oc)])
    arrived("Xx0", x2t.at[slot(od, oh, c)])
    arrived("Xx1", x2t.at[slot(od, oh, oc)])
    arrived("Xa2", x2t.at[slot(d, oh, c)])
    arrived("Xb2", x2t.at[slot(d, oh, oc)])
    arrived("Fi0", piece(slot(od, h, oc), 0))
    tiles(0)
    pass_on("Fx1", "Gx1", piece(slot(od, oh, c), 1))
    send("Gb", quarter(slot(od, oh, c), 0), quarter(slot(od, oh, c), 0), intra)
    reduce_2(0)
    send("Pd0", pbuf.at[d, 2 * oh + c], arel.at[0], intra)
    send("Pa", pbuf.at[d, 2 * h + oc], actr.at[me], sibling)

    pass_on("Fi1", "Gi1", piece(slot(od, h, c), 1))
    send("Ga2", quarter(slot(od, h, c), 1), quarter(slot(od, h, c), 1), inter)
    send("Pd1", pbuf.at[d, 2 * oh + oc], arel.at[1], inter)
    arrived("Fi1", piece(slot(od, h, oc), 1))
    tiles(1)
    reduce_3(0)
    act_part(od, 0, 2)
    reduce_2(1)
    pass_on("Fx0", "Gx0", piece(slot(od, oh, c), 0))
    act_part(od, 2, 4)
    reduce_4(0)
    act_part(od, 4, 6)
    pass_on("Fb", "Gb", quarter(slot(d, oh, c), 0))
    act_part(od, 6, 8)
    send("Pb0", pbuf.at[od, 2 * h + c], actr.at[me], intra)
    send("Pb1", pbuf.at[od, 2 * h + oc], actr.at[me], intra_o)
    send("Pc0", pbuf.at[od, 2 * oh + c], actr.at[me], inter)
    send("Pc1", pbuf.at[od, 2 * oh + oc], actr.at[me], inter_o)
    pass_on("Fa", "Ga", piece(slot(d, oh, c), 0))
    arrived("Fx0", piece(slot(od, oh, oc), 0))
    arrived("Fa", piece(slot(d, oh, oc), 0))
    tiles(2)
    pass_on("Fa2", "Ga2", quarter(slot(d, oh, c), 1))
    arrived("Fx1", piece(slot(od, oh, oc), 1))
    arrived("Fb", quarter(slot(d, oh, oc), 0))
    arrived("Fa2", quarter(slot(d, oh, oc), 1))
    grad_tile(3, across(z), across(y))
    reduce_1(3)
    reduce_3(1)
    reduce_2(2)
    hand_over(0)
    grad_tile(3, up(z), up(y))
    grad_tile(3, down(z), down(y))
    grad_tile(3, z, y)
    reduce_2(3)
    reduce_4(1)
    arrived("Pd1", arel.at[1])
    send("Pf1", arel.at[1], actr.at[slot(od, oh, c)], intra_o)
    arrived("Pd0", arel.at[0])
    send("Pf0", arel.at[0], actr.at[slot(od, h, c)], inter)
    reduce_3(2)
    hand_over(1)
    reduce_4(2)
    in_ma.wait()
    in_mo.wait()
    in_se.wait()
    hand_over(2)
    reduce_3(3)
    reduce_4(3)
    hand_over(3)
    update(0)
    update(1)

    arrived("Pa", actr.at[slot(d, h, oc)])
    arrived("Pb0", actr.at[slot(od, h, c)])
    arrived("Pb1", actr.at[slot(od, h, oc)])
    arrived("Pc0", actr.at[slot(od, oh, c)])
    arrived("Pc1", actr.at[slot(od, oh, oc)])
    arrived("Pf0", actr.at[slot(d, oh, c)])
    arrived("Pf1", actr.at[slot(d, oh, oc)])
    actr[me] = pbuf[d, m]
    for p in range(4):
        k = 4 * (p // 2) + p % 2
        both = wide(actr[k]) + wide(actr[k + 2])
        rbuf[p * 128:(p + 1) * 128, :] = both.astype(BF16)
        bsend[p:p + 1, :] = both[0:1]
    send("bnd", bsend, brecv, prev_dev)
    arrived("bnd", brecv)
    for j in range(2):
        arrived("nw" + str(j), nw.at[od, :, span[j]])
    for mine, copy in maybe:

        @pl.when(jnp.logical_not(mine))
        def _():
            copy.wait_send()

    for copy in sent:
        copy.wait_send()


def finish(r_ref, b_ref, ma, mo, se, nw, act_out, nm_out, nmo_out, ns_out, nw_out, act, act_sem, sem):
    copies = [
        pltpu.make_async_copy(src, dst, sem.at[i])
        for i, (src, dst) in enumerate(((ma, nm_out), (mo, nmo_out), (se, ns_out), (nw, nw_out)))
    ]
    for copy in copies:
        copy.start()
    last = lax.axis_index("seq") * 4 + lax.axis_index("mp") == 63
    rows = lax.broadcasted_iota(jnp.int32, (512, 512), 0)
    cols = lax.broadcasted_iota(jnp.int32, (512, 512), 1)
    put = jnp.where(rows == 4 * (cols % 128) + cols // 128 - 3, 1.0, 0.0).astype(BF16)
    line = lax.broadcasted_iota(jnp.int32, (16, 512), 0)
    for t in range(4):
        span = pl.ds(t * 512, 512)
        out = jnp.dot(put, r_ref[:, span], preferred_element_type=F32)
        act[0:496, span] = out[0:496].astype(BF16)
        tail = out[496:512]
        for p in range(3):
            row = jnp.where(last, 0.0, b_ref[p:p + 1, span])
            tail = jnp.where(line == 13 + p, row, tail)
        act[496:512, span] = tail.astype(BF16)
        copy = pltpu.make_async_copy(act.at[:, span], act_out.at[:, span], act_sem.at[t])
        copy.start()
        copies.append(copy)
    for copy in copies:
        copy.wait()


def per_device(shortening_input, coarse_grad, weight_copy, master, moment, second):
    x = shortening_input[0]
    g = coarse_grad[0]
    fine, features = x.shape
    width = g.shape[1]
    w = weight_copy.reshape(2, features, width)
    rows = master.shape[1]
    scale = 1.0 / math.sqrt(lax.axis_size("dp") * lax.axis_size("seq") * g.shape[0])
    any_spec = pl.BlockSpec(memory_space=pl.ANY)
    vm = pltpu.VMEM
    held = pl.pallas_call(
        functools.partial(kernel, scale),
        out_shape=(
            vm((fine, features), BF16),
            vm((4, features), F32),
            vm((rows, width), F32),
            vm((rows, width), F32),
            vm((rows, width), F32),
            vm((2, rows, width), BF16),
        ),
        in_specs=[any_spec] * 6,
        out_specs=[pl.BlockSpec(memory_space=pltpu.VMEM)] * 6,
        scratch_shapes=[
            vm((512, 2048), BF16),
            vm((8, 4, 4, 64, 128), BF16),
            vm((8, 4, 4, 64, 128), BF16),
            vm((2, 4, 4, 64, 128), BF16),
            vm((8, 512, 1024), BF16),
            vm((2048, 1024), BF16),
            vm((2048, 1024), BF16),
            vm((2, 4, 128, 2048), BF16),
            vm((8, 128, 2048), BF16),
            vm((2, 128, 2048), BF16),
            vm((4, 2, 4, 4, 64, 512), BF16),
            vm((4, 2, 2, 2, 64, 512), BF16),
            vm((4, 2, 2, 4, 64, 512), BF16),
            vm((4, 2, 4, 64, 512), BF16),
            vm((4, 2, 2, 32, 512), BF16),
            vm((4, 2, 2, 64, 512), BF16),
            vm((4, 2, 64, 512), BF16),
            vm((4, 2, 64, 512), BF16),
            vm((4, 2048), F32),
            pltpu.SemaphoreType.DMA((COPIES,)),
            pltpu.SemaphoreType.DMA((COPIES,)),
            pltpu.SemaphoreType.DMA((LOCALS,)),
        ],
        compiler_params=pltpu.CompilerParams(
            collective_id=0, has_side_effects=True, vmem_limit_bytes=57_500_000
        ),
    )(x, g, w, master[0], moment[0], second[0])
    act, new_master, new_moment, new_second, new_weight = pl.pallas_call(
        finish,
        out_shape=(
            jax.ShapeDtypeStruct((fine, features), BF16),
            jax.ShapeDtypeStruct((rows, width), F32),
            jax.ShapeDtypeStruct((rows, width), F32),
            jax.ShapeDtypeStruct((rows, width), F32),
            jax.ShapeDtypeStruct((2, rows, width), BF16),
        ),
        in_specs=[pl.BlockSpec(memory_space=pltpu.VMEM)] * 2 + [any_spec] * 4,
        out_specs=[any_spec] * 5,
        scratch_shapes=[
            vm((fine, features), BF16),
            pltpu.SemaphoreType.DMA((4,)),
            pltpu.SemaphoreType.DMA((4,)),
        ],
        compiler_params=pltpu.CompilerParams(vmem_limit_bytes=16_000_000),
    )(*held)
    return (act[None], new_master[None], new_moment[None], new_second[None], new_weight)


def solution(mesh):
    return jax.shard_map(
        per_device,
        mesh=mesh,
        in_specs=(
            P("dp", ("seq", "mp"), None),
            P("dp", "seq", "mp"),
            P("dp", None, "mp"),
            P("dp", "seq", "mp"),
            P("dp", "seq", "mp"),
            P("dp", "seq", "mp"),
        ),
        out_specs=(
            P("dp", ("seq", "mp"), None),
            P("dp", "seq", "mp"),
            P("dp", "seq", "mp"),
            P("dp", "seq", "mp"),
            P(None, "seq", "mp"),
        ),
        check_vma=False,
    )
```
